32 devices in a mesh: req: 16 (over z, x, core), tp: 2 (over y).
Axes of the slice: x: 2, y: 2, z: 4, core: 2. Of those that a mesh axis runs over, the one named last changes fastest.
Arguments:
- decode_tokens: bfloat16 [128, 2048], P('req', 'tp'), may hold values from -6 to 6
- prefill_tokens: bfloat16 [8192, 2048], P('req', 'tp'), may hold values from -6 to 6
- qkv_weight: bfloat16 [2048, 3, 8, 128], P(None, None, 'tp'), may hold values from -0.125 to 0.125
- out_weight: bfloat16 [8, 128, 2048], P('tp'), may hold values from -0.1875 to 0.1875
- prefix_cache: bfloat16 [16, 2048, 8, 2, 128], P('req', None, 'tp'), may hold values from -70 to 70
- page_pool: bfloat16 [256, 128, 8, 2, 128], P('req', None, 'tp'), may hold values from -70 to 70
- page_table: int32 [128, 2], P('req'), may hold values from 0 to 15, as said below
- cached_len: int32 [128], P('req'), may hold values from 1 to 256, as said below
- group_sizes: int32 [16], replicated, may hold values from 1 to 16, 128 in all
- member_order: int32 [128], replicated, may hold values from 0 to 127, each once
- span_start: int32 [16], P('req'), may hold values from 1 to 2048
Outputs:
- decode_out: bfloat16 [128, 2048], P('req', 'tp')
- prefill_out: bfloat16 [8192, 2048], P('req', 'tp')
The draws below stay inside these ranges and needn't reach their ends.
Inputs may be any that keep to these rules, and one draw needn't show every extreme that they name: `page_table`: the 2 entries of the 8 requests of one index of req name each of that index's 16 pool slots once. `cached_len`: on every index of req one request has exactly 256 private tokens. `group_sizes`: the sizes sum to 128; some group has exactly 16 requests.
All inputs are finite; a program needn't handle non-finite values.
Results may differ from the reference program's by a relative error of at most 0.012.
The reference program's roundings to bfloat16 on the way (of `normed`) count: a program that leaves them out, or rounds other values in their place, can miss the bound.
Values may be sent and summed in bfloat16 or wider, within the bound.
A program may use at most 128 MiB of HBM per device.

```python
import math
import jax
import jax.numpy as jnp
import numpy as np
from jax import lax

D = 2048
HEAD_DIM = 128
HEADS = 8
PAGE = 128
PREF = 2048
MAXP = 2
SPAN = 512
DEC_DEV = 8
GMAX = 16
DECODES = 128
GROUPS = 16
PRE_TOK = 8192
POOL_DEV = 16
POOLS = 256
N_REQ = 16


def cache_values(key, shape):
    return jnp.clip(jax.random.normal(key, shape, jnp.float32), -6.0, 6.0)


def draw_prefix_cache(key, part):
    return cache_values(jax.random.fold_in(key, 11), (GROUPS, PREF, HEADS, 2, HEAD_DIM)).astype(jnp.bfloat16)


def draw_page_pool(key, part):
    return cache_values(jax.random.fold_in(key, 12), (POOLS, PAGE, HEADS, 2, HEAD_DIM)).astype(jnp.bfloat16)


def draw_page_table(key, part):
    devices = DECODES // DEC_DEV
    keys = jax.random.split(jax.random.fold_in(key, 13), devices)
    orders = jax.vmap(lambda single: jax.random.permutation(single, POOL_DEV))(keys)
    return orders.reshape(DECODES, MAXP).astype(jnp.int32)


def draw_cached_len(key, part):
    devices = DECODES // DEC_DEV
    first, second = jax.random.split(jax.random.fold_in(key, 14))
    base = jax.random.randint(first, (devices, DEC_DEV), 1, MAXP * PAGE + 1)
    picked = jax.random.randint(second, (devices, 1), 0, DEC_DEV)
    longest = jnp.where(jnp.arange(DEC_DEV)[None, :] == picked, MAXP * PAGE, base)
    return longest.reshape(DECODES).astype(jnp.int32)


def touch_ends(values, rng, low, high):
    longest = values.shape.index(max(values.shape))
    spots = []
    for shift in (0, 1):
        where = [jax.random.randint(jax.random.fold_in(rng, axis), (), 0, length) for axis, length in enumerate(values.shape)]
        where[longest] = (where[longest] + shift) % values.shape[longest]
        spots.append(tuple(where))
    return values.at[spots[0]].set(low).at[spots[1]].set(high)


def levels(key, shape, cuts, smallest, high):
    factor_of, own = 1.0, jax.random.fold_in(key, 6)
    for dim, shards_of in cuts:
        steps = jnp.exp(jax.random.uniform(jax.random.fold_in(own, dim), (shards_of,), jnp.float32, smallest / len(cuts), high / len(cuts)))
        factor_of = factor_of * jnp.repeat(steps, shape[dim] // shards_of).reshape([-1 if axis == dim else 1 for axis in range(len(shape))])
    return factor_of


def length_profile(amount, total, bound, skew):
    portions = [(1 << 20) // math.isqrt(grade ** skew) + 1 for grade in range(2, amount + 1)]
    spare, given = total - bound - (amount - 1), [1] * (amount - 1)
    while spare > 0:
        candidates = [i for i in range(amount - 1) if given[i] < bound]
        pool, remaining = sum([portions[i] for i in candidates]), spare
        for i in candidates:
            extra = min(bound - given[i], max(1, remaining * portions[i] // pool), spare)
            given[i] = given[i] + extra
            spare = spare - extra
    return np.array([bound] + given)


def ragged(stream_key, amount, total, reach, slope):
    if amount == 2:
        one = jax.random.randint(stream_key, (), max(1, total - reach), min(reach, total - 1) + 1)
        return jnp.stack([one, total - one])
    tallies = jnp.asarray(length_profile(amount, total, reach, slope), jnp.int32)
    couples = (amount - 1) // 2
    giver, taker = tallies[1:1 + 2 * couples:2], tallies[2:2 + 2 * couples:2]
    margin = jnp.minimum(giver - 1, reach - taker)
    moved = jax.random.randint(jax.random.fold_in(stream_key, 1), (couples,), 0, 1 << 20) % (margin + 1)
    tallies = tallies.at[1:1 + 2 * couples:2].set(giver - moved).at[2:2 + 2 * couples:2].set(taker + moved)
    return tallies[jax.random.permutation(jax.random.fold_in(stream_key, 2), amount)]


def bell_draw(own_key, shape, scale, reach, cuts=(), kind=jnp.bfloat16):
    gain = levels(own_key, shape, cuts, -0.22, 0.18) if cuts else 1.0
    drawn = jax.random.normal(own_key, shape, jnp.float32) * scale * gain
    return jnp.minimum(jnp.maximum(drawn, -reach), reach).astype(kind)


def setup_inputs(seed: int = 0) -> dict:
    arg_keys = jax.random.split(jax.random.key(seed), 12)
    return {
        "decode_tokens": bell_draw(arg_keys[0], (DECODES, D), 1.0, 6.0, ((0, 16), (1, 2))),
        "prefill_tokens": bell_draw(arg_keys[1], (PRE_TOK, D), 1.0, 6.0, ((0, 16), (1, 2))),
        "qkv_weight": bell_draw(arg_keys[2], (D, 3, HEADS, HEAD_DIM), D ** -0.5, 0.125, ((2, 2),)),
        "out_weight": bell_draw(arg_keys[3], (HEADS, HEAD_DIM, D), (HEADS * HEAD_DIM) ** -0.5, 0.1875, ((0, 2),)),
        "prefix_cache": draw_prefix_cache(jax.random.fold_in(arg_keys[11], 71), 0),
        "page_pool": draw_page_pool(jax.random.fold_in(arg_keys[11], 71), 0),
        "page_table": draw_page_table(jax.random.fold_in(arg_keys[11], 71), 0),
        "cached_len": draw_cached_len(jax.random.fold_in(arg_keys[11], 71), 0),
        "group_sizes": ragged(arg_keys[8], GROUPS, DECODES, GMAX, 2).astype(jnp.int32),
        "member_order": jax.random.permutation(arg_keys[9], DECODES).astype(jnp.int32),
        "span_start": touch_ends(jax.random.randint(arg_keys[10], (GROUPS,), 1, PREF + 1), jax.random.fold_in(arg_keys[10], 1), 1, PREF).astype(jnp.int32),
    }


def norm_rows(values):
    wide = values.astype(jnp.float32)
    centre = lax.optimization_barrier(jnp.mean(wide, axis=-1, keepdims=True))
    spread = lax.optimization_barrier(jnp.mean((wide - centre) ** 2, axis=-1, keepdims=True))
    return ((wide - centre) * lax.rsqrt(spread + 1e-05)).astype(jnp.bfloat16)

def rotary(values, places):
    half_dim = values.shape[-1] // 2
    inverse = 10000.0 ** (-(jnp.arange(half_dim, dtype=jnp.float32) / half_dim))
    angles = places.astype(jnp.float32)[:, None] * inverse[None, :]
    cosine = jnp.cos(angles)[:, None, :]
    sine = jnp.sin(angles)[:, None, :]
    first = values[..., :half_dim]
    second = values[..., half_dim:]
    return jnp.concatenate([first * cosine - second * sine, second * cosine + first * sine], axis=-1)

def project(normed, weight):
    flat = weight.reshape(weight.shape[0], -1)
    mixed = jnp.dot(normed, flat, preferred_element_type=jnp.float32)
    return mixed.reshape(normed.shape[0], 3, weight.shape[2], weight.shape[3])

def reference(decode_tokens, prefill_tokens, qkv_weight, out_weight, prefix_cache, page_pool, page_table, cached_len, group_sizes, member_order, span_start):
    score_scale = HEAD_DIM ** (-0.5)
    dec_qkv = project(norm_rows(decode_tokens), qkv_weight)
    pre_qkv = project(norm_rows(prefill_tokens), qkv_weight)
    dec_places = (PREF + cached_len).astype(jnp.int32)
    dec_query = rotary(dec_qkv[:, 0], dec_places).astype(jnp.bfloat16)
    dec_key = rotary(dec_qkv[:, 1], dec_places).astype(jnp.bfloat16)
    dec_value = dec_qkv[:, 2].astype(jnp.bfloat16)
    pre_places = (span_start[:, None] + jnp.arange(SPAN, dtype=jnp.int32)[None, :]).reshape(-1).astype(jnp.int32)
    pre_query = rotary(pre_qkv[:, 0], pre_places).astype(jnp.bfloat16)
    pre_key = rotary(pre_qkv[:, 1], pre_places).astype(jnp.bfloat16)
    pre_value = pre_qkv[:, 2].astype(jnp.bfloat16)
    group_ends = jnp.cumsum(group_sizes).astype(jnp.int32)
    ranks = jnp.arange(DECODES, dtype=jnp.int32)
    rank_group = lax.optimization_barrier(jnp.sum((ranks[:, None] >= group_ends[None, :]).astype(jnp.int32), axis=1)).astype(jnp.int32)
    row_group = jnp.zeros((DECODES,), jnp.int32).at[member_order].set(rank_group)

    def one_decode(items):
        query, key_new, value_new, group, row, table_row, length = items
        query_wide = query.astype(jnp.float32)
        prefix = lax.dynamic_index_in_dim(prefix_cache, group, 0, keepdims=False)
        far_scores = jnp.einsum('hd,phd->hp', query_wide, prefix[:, :, 0].astype(jnp.float32)) * score_scale
        far_peak = lax.optimization_barrier(jnp.max(far_scores, axis=-1))
        far_weights = jnp.exp(far_scores - far_peak[:, None])
        far_total = lax.optimization_barrier(jnp.sum(far_weights, axis=-1))
        far_numer = jnp.einsum('hp,phd->hd', far_weights.astype(jnp.bfloat16).astype(jnp.float32), prefix[:, :, 1].astype(jnp.float32))
        slots = (row // DEC_DEV * POOL_DEV + table_row).astype(jnp.int32)
        pages = page_pool[slots].reshape(MAXP * PAGE, HEADS, 2, HEAD_DIM)
        near_scores = jnp.einsum('hd,thd->ht', query_wide, pages[:, :, 0].astype(jnp.float32)) * score_scale
        valid = jnp.arange(MAXP * PAGE, dtype=jnp.int32) < length
        near_scores = jnp.where(valid[None, :], near_scores, -1e+30)
        own_score = lax.optimization_barrier(jnp.sum(query_wide * key_new.astype(jnp.float32), axis=-1)) * score_scale
        near_peak = jnp.maximum(lax.optimization_barrier(jnp.max(near_scores, axis=-1)), own_score)
        near_weights = jnp.where(valid[None, :], jnp.exp(near_scores - near_peak[:, None]), 0.0)
        own_weight = jnp.exp(own_score - near_peak)
        near_total = lax.optimization_barrier(jnp.sum(near_weights, axis=-1)) + own_weight
        near_numer = jnp.einsum('ht,thd->hd', near_weights.astype(jnp.bfloat16).astype(jnp.float32), pages[:, :, 1].astype(jnp.float32))
        near_numer = near_numer + own_weight.astype(jnp.bfloat16).astype(jnp.float32)[:, None] * value_new.astype(jnp.float32)
        top = jnp.maximum(far_peak, near_peak)
        far_factor = jnp.exp(far_peak - top)
        near_factor = jnp.exp(near_peak - top)
        merged = (far_factor[:, None] * far_numer + near_factor[:, None] * near_numer) / (far_factor * far_total + near_factor * near_total)[:, None]
        return merged.astype(jnp.bfloat16)
    row_index = jnp.arange(DECODES, dtype=jnp.int32)
    dec_context = lax.map(one_decode, (dec_query, dec_key, dec_value, row_group, row_index, page_table, cached_len))

    def one_span(items):
        query, key_new, value_new, prefix, start = items
        keys_all = jnp.concatenate([prefix[:, :, 0], key_new], axis=0).astype(jnp.float32)
        values_all = jnp.concatenate([prefix[:, :, 1], value_new], axis=0).astype(jnp.float32)
        scores = jnp.einsum('qhd,khd->hqk', query.astype(jnp.float32), keys_all) * score_scale
        key_places = jnp.arange(PREF + SPAN, dtype=jnp.int32)
        row_places = jnp.arange(SPAN, dtype=jnp.int32)
        allowed = jnp.where(key_places[None, :] < PREF, key_places[None, :] < start, key_places[None, :] - PREF <= row_places[:, None])
        scores = jnp.where(allowed[None], scores, -1e+30)
        peak = lax.optimization_barrier(jnp.max(scores, axis=-1))
        weights = jnp.where(allowed[None], jnp.exp(scores - peak[..., None]), 0.0)
        total = lax.optimization_barrier(jnp.sum(weights, axis=-1))
        numer = jnp.einsum('hqk,khd->qhd', weights.astype(jnp.bfloat16).astype(jnp.float32), values_all)
        return (numer / jnp.transpose(total)[:, :, None]).astype(jnp.bfloat16)
    pre_context = lax.map(one_span, (pre_query.reshape(N_REQ, SPAN, HEADS, HEAD_DIM), pre_key.reshape(N_REQ, SPAN, HEADS, HEAD_DIM), pre_value.reshape(N_REQ, SPAN, HEADS, HEAD_DIM), prefix_cache, span_start))
    flat_out = out_weight.reshape(HEADS * HEAD_DIM, D)
    decode_out = jnp.dot(dec_context.reshape(DECODES, HEADS * HEAD_DIM), flat_out, preferred_element_type=jnp.float32).astype(jnp.bfloat16)
    prefill_out = jnp.dot(pre_context.reshape(PRE_TOK, HEADS * HEAD_DIM), flat_out, preferred_element_type=jnp.float32).astype(jnp.bfloat16)
    return (decode_out, prefill_out)
```

```python
import functools
import math

import jax
import jax.numpy as jnp
from jax import lax
from jax.experimental import pallas as pl
from jax.experimental.pallas import tpu as pltpu
from jax.sharding import PartitionSpec as P

GMAX = 16
F32, BF16 = jnp.float32, jnp.bfloat16
MESH = pl.DeviceIdType.MESH
VM = pl.BlockSpec(memory_space=pltpu.VMEM)
SM = pl.BlockSpec(memory_space=pltpu.SMEM)
BIG = 56 << 20


def dot(a, b):
    return jnp.dot(a, b, preferred_element_type=F32)


def dot_t(a, b):
    return lax.dot_general(a, b, (((1,), (1,)), ((), ())), preferred_element_type=F32)


def spread_rows(src, dst, tokens, group):
    piece = 16
    while piece * 2 * group <= 256 and piece * 2 <= tokens:
        piece *= 2
    rows = piece * group
    at = lax.broadcasted_iota(jnp.int32, (rows, rows), 0)
    col = lax.broadcasted_iota(jnp.int32, (rows, rows), 1)
    shift = piece.bit_length() - 1
    want = (at & (piece - 1)) * group + lax.shift_right_logical(at, shift)
    pick = jnp.where(col == want, 1.0, 0.0).astype(BF16)
    for k in range(tokens // piece):
        moved = dot(pick, src[k * rows : (k + 1) * rows, :]).astype(BF16)
        for g in range(group):
            dst[k * piece : (k + 1) * piece, g * 128 : (g + 1) * 128] = moved[
                g * piece : (g + 1) * piece, :
            ]


def prep_kernel(groups, tokens, *refs):
    half = len(refs) // 2
    for src, dst, g in zip(refs[:half], refs[half:], groups):
        spread_rows(src, dst, tokens, g)


def prep(arrays, groups, total):
    steps = 16
    tokens = total // steps
    return pl.pallas_call(
        functools.partial(prep_kernel, groups, tokens),
        grid=(steps,),
        out_shape=[jax.ShapeDtypeStruct((total, g * 128), BF16) for g in groups],
        in_specs=[pl.BlockSpec((tokens * g, 128), lambda i: (i, 0)) for g in groups],
        out_specs=[pl.BlockSpec((tokens, g * 128), lambda i: (i, 0)) for g in groups],
        compiler_params=pltpu.CompilerParams(vmem_limit_bytes=BIG),
        cost_estimate=pl.CostEstimate(
            flops=int(2e9), bytes_accessed=int(4 * total * 128 * sum(groups)), transcendentals=0
        ),
        name="prep",
    )(*arrays)


def gather_kernel(axis, count, x_ref, out_ref, send, recv):
    me = lax.axis_index(axis)
    barrier = pltpu.get_barrier_semaphore()

    def greet(k, _):
        pl.semaphore_signal(
            barrier, inc=1, device_id={axis: lax.rem(me + k, count)}, device_id_type=MESH
        )
        return 0

    lax.fori_loop(1, count, greet, 0)
    pl.semaphore_wait(barrier, count - 1)

    def make(k):
        return pltpu.make_async_remote_copy(
            src_ref=x_ref,
            dst_ref=out_ref.at[me],
            send_sem=send.at[k],
            recv_sem=recv.at[k],
            device_id={axis: lax.rem(me + k, count)},
            device_id_type=MESH,
        )

    def go(k, _):
        make(k).start()
        return 0

    lax.fori_loop(1, count, go, 0)
    out_ref[me] = x_ref[...]

    def done(k, _):
        make(k).wait()
        return 0

    lax.fori_loop(1, count, done, 0)


def gather_all(x, axis, count, ident):
    return pl.pallas_call(
        functools.partial(gather_kernel, axis, count),
        out_shape=jax.ShapeDtypeStruct((count,) + x.shape, x.dtype),
        in_specs=[VM],
        out_specs=VM,
        scratch_shapes=[pltpu.SemaphoreType.DMA((count,)), pltpu.SemaphoreType.DMA((count,))],
        compiler_params=pltpu.CompilerParams(collective_id=ident, has_side_effects=True),
        name="gather_all",
    )(x)


def normed_parts(parts):
    wide = [p.astype(F32) for p in parts]
    width = sum(p.shape[1] for p in parts)
    centre = sum(jnp.sum(w, axis=1, keepdims=True) for w in wide) * (1.0 / width)
    moved = [w - centre for w in wide]
    spread = sum(jnp.sum(m * m, axis=1, keepdims=True) for m in moved) * (1.0 / width)
    gain = lax.rsqrt(spread + 1e-05)
    return [(m * gain).astype(BF16) for m in moved]


def qkv_rows(parts, offs, w_ref):
    out = None
    for k, part in enumerate(normed_parts(parts)):
        depth = part.shape[1]
        rows = w_ref[pl.ds(pl.multiple_of(offs[k], 128), depth), :]
        term = dot(part, rows)
        out = term if out is None else out + term
    return out


def turn(y, cos, sin):
    return y * cos + pltpu.roll(y, 64, 1) * sin


def dec_qkv_kernel(n, heads, offs, *refs):
    parts = [r[...] for r in refs[:n]]
    w_ref, cos, sin, q_out, k_out, v_out = refs[n:]
    y = qkv_rows(parts, [offs[k] for k in range(n)], w_ref)
    c, s = cos[...], sin[...]
    for h in range(heads):
        here = slice(h * 128, (h + 1) * 128)
        q_out[:, here] = turn(y[:, h * 128 : (h + 1) * 128], c, s).astype(BF16)
        k_out[:, here] = turn(
            y[:, (heads + h) * 128 : (heads + h + 1) * 128], c, s
        ).astype(BF16)
        v_out[:, here] = y[:, (2 * heads + h) * 128 : (2 * heads + h + 1) * 128].astype(BF16)


def dec_attn_kernel(heads, scale, allq, members, prefix, q, knew, vnew, pool, table, lens, far, near):
    every = allq.shape[0]
    sel = jnp.where(
        members[...] == lax.broadcasted_iota(jnp.int32, (GMAX, every), 1), 1.0, 0.0
    ).astype(BF16)
    chosen = dot(sel, allq[...]).astype(BF16)
    rows = q.shape[0]
    slots = pool.shape[0]
    t = lax.broadcasted_iota(jnp.int32, (rows, slots), 1)
    page, off = lax.shift_right_logical(t, 7), t & 127
    valid = None
    for j in range(table.shape[1]):
        one = (page == table[:, j : j + 1]) & (off + j * 128 < lens[...])
        valid = one if valid is None else valid | one
    lane_f = lax.broadcasted_iota(jnp.int32, (GMAX, 128), 1)
    lane_n = lax.broadcasted_iota(jnp.int32, (rows, 128), 1)
    far_stat = jnp.zeros((GMAX, 128), F32)
    near_stat = jnp.zeros((rows, 128), F32)
    for h in range(heads):
        here = slice(h * 128, (h + 1) * 128)
        kcol = slice(h * 256, h * 256 + 128)
        vcol = slice(h * 256 + 128, h * 256 + 256)
        s = dot_t(chosen[:, here], prefix[:, kcol]) * scale
        m = jnp.max(s, axis=1, keepdims=True)
        w = jnp.exp(s - m)
        far_stat = jnp.where(lane_f == h, m, far_stat)
        far_stat = jnp.where(
            lane_f == heads + h, jnp.sum(w, axis=1, keepdims=True), far_stat
        )
        far[:, here] = dot(w.astype(BF16), prefix[:, vcol])
        qh = q[:, here]
        s = jnp.where(valid, dot_t(qh, pool[:, kcol]) * scale, -1e30)
        own = (
            jnp.sum(qh.astype(F32) * knew[:, here].astype(F32), axis=1, keepdims=True) * scale
        )
        m = jnp.maximum(jnp.max(s, axis=1, keepdims=True), own)
        w = jnp.where(valid, jnp.exp(s - m), 0.0)
        ow = jnp.exp(own - m)
        near_stat = jnp.where(lane_n == h, m, near_stat)
        near_stat = jnp.where(
            lane_n == heads + h, jnp.sum(w, axis=1, keepdims=True) + ow, near_stat
        )
        near[:, here] = dot(w.astype(BF16), pool[:, vcol]) + ow.astype(BF16).astype(
            F32
        ) * vnew[:, here].astype(F32)
    far[:, heads * 128 :] = far_stat
    near[:, heads * 128 :] = near_stat


def merge_kernel(heads, base, got, owners, near, ctx):
    rows = near.shape[0]
    slots = got.shape[0]
    want = base[0] + lax.broadcasted_iota(jnp.int32, (rows, slots), 0)
    pick = jnp.where(owners[...] == want, 1.0, 0.0)
    far = jnp.dot(
        pick, got[...], preferred_element_type=F32, precision=lax.Precision.HIGHEST
    )
    fs, ns = far[:, heads * 128 :], near[:, heads * 128 :]
    for h in range(heads):
        here = slice(h * 128, (h + 1) * 128)
        mp, lp = fs[:, h : h + 1], fs[:, heads + h : heads + h + 1]
        ml, ll = ns[:, h : h + 1], ns[:, heads + h : heads + h + 1]
        top = jnp.maximum(mp, ml)
        a, b = jnp.exp(mp - top), jnp.exp(ml - top)
        ctx[:, here] = (
            (a * far[:, here] + b * near[:, here]) / (a * lp + b * ll)
        ).astype(BF16)


def prefill_kernel(n, heads, rows, scale, scal, *refs):
    parts = [r[...] for r in refs[:n]]
    w_ref, cos, sin, prefix, ctx, kself, vself = refs[n:]
    step = pl.program_id(0)
    start = scal[n]

    @pl.when(step == 0)
    def _():
        kself[...] = jnp.zeros_like(kself)
        vself[...] = jnp.zeros_like(vself)

    y = qkv_rows(parts, [scal[k] for k in range(n)], w_ref)
    c, s = cos[...], sin[...]
    at = pl.ds(pl.multiple_of(step * rows, rows), rows)
    total = kself.shape[0]
    far_len = prefix.shape[0]
    far_bias = jnp.where(
        lax.broadcasted_iota(jnp.int32, (1, far_len), 1) < start, 0.0, -1e30
    )
    near_ok = lax.broadcasted_iota(jnp.int32, (rows, total), 1) <= (
        step * rows + lax.broadcasted_iota(jnp.int32, (rows, total), 0)
    )
    factor = scale * math.log2(math.e)
    for h in range(heads):
        here = slice(h * 128, (h + 1) * 128)
        kcol = slice(h * 256, h * 256 + 128)
        vcol = slice(h * 256 + 128, h * 256 + 256)
        qh = turn(y[:, h * 128 : (h + 1) * 128], c, s).astype(BF16)
        kself[at, here] = turn(
            y[:, (heads + h) * 128 : (heads + h + 1) * 128], c, s
        ).astype(BF16)
        vself[at, here] = y[:, (2 * heads + h) * 128 : (2 * heads + h + 1) * 128].astype(BF16)
        sf = dot_t(qh, prefix[:, kcol]) + far_bias
        sn = jnp.where(near_ok, dot_t(qh, kself[:, here]), -1e30)
        m = jnp.maximum(
            jnp.max(sf, axis=1, keepdims=True), jnp.max(sn, axis=1, keepdims=True)
        )
        wf = jnp.exp2((sf - m) * factor)
        wn = jnp.exp2((sn - m) * factor)
        l = jnp.sum(wf, axis=1, keepdims=True) + jnp.sum(wn, axis=1, keepdims=True)
        o = dot(wf.astype(BF16), prefix[:, vcol]) + dot(wn.astype(BF16), vself[:, here])
        ctx[:, here] = (o / l).astype(BF16)


def out_kernel(n, *refs):
    ctxs, decs, ws = refs[:n], refs[n : 2 * n], refs[2 * n : 3 * n]
    pre_out, dec_out = refs[3 * n :]
    pre_out[...] = sum(dot(c[...], w[...]) for c, w in zip(ctxs, ws)).astype(pre_out.dtype)

    @pl.when(pl.program_id(0) == 0)
    def _():
        dec_out[...] = sum(dot(c[...], w[...]) for c, w in zip(decs, ws)).astype(dec_out.dtype)


def tables(places):
    inverse = 10000.0 ** (-(jnp.arange(64, dtype=F32) / 64))
    angles = places.astype(F32)[:, None] * inverse[None, :]
    c, s = jnp.cos(angles), jnp.sin(angles)
    return jnp.concatenate([c, c], axis=1), jnp.concatenate([-s, s], axis=1)


def local(
    n_req,
    n_tp,
    decode_tokens,
    prefill_tokens,
    qkv_weight,
    out_weight,
    prefix_cache,
    page_pool,
    page_table,
    cached_len,
    group_sizes,
    member_order,
    span_start,
):
    heads = qkv_weight.shape[2]
    width = heads * 128
    features = qkv_weight.shape[0]
    scale = 128 ** (-0.5)
    prefix_len = prefix_cache.shape[1]
    block_rows, share = prefill_tokens.shape
    dec_count = decode_tokens.shape[0]
    me = lax.axis_index("req")
    side = lax.axis_index("tp")
    swap = [(0, 1), (1, 0)]
    if n_tp == 2:
        dec_parts = [decode_tokens, lax.ppermute(decode_tokens, "tp", swap)]
        pre_parts = [prefill_tokens, lax.ppermute(prefill_tokens, "tp", swap)]
        offs = [side * share, (1 - side) * share]
    else:
        dec_parts = [lax.all_gather(decode_tokens, "tp", axis=1, tiled=True)]
        pre_parts = [lax.all_gather(prefill_tokens, "tp", axis=1, tiled=True)]
        offs = [jnp.int32(0)]
    n = len(offs)
    slots = page_pool.shape[0] * page_pool.shape[1]
    weight, prefix, pool = prep(
        [
            qkv_weight.reshape(-1, 128),
            prefix_cache.reshape(-1, 128),
            page_pool.reshape(-1, 128),
        ],
        [3 * heads, 2 * heads, 2 * heads],
        features,
    ) if features == prefix_len == slots else (
        prep([qkv_weight.reshape(-1, 128)], [3 * heads], features)
        + prep([prefix_cache.reshape(-1, 128)], [2 * heads], prefix_len)
        + prep([page_pool.reshape(-1, 128)], [2 * heads], slots)
    )
    begin = jnp.cumsum(group_sizes) - group_sizes
    slot_at = jnp.arange(GMAX, dtype=jnp.int32)[None, :]
    padded = jnp.concatenate([member_order, jnp.zeros((GMAX,), jnp.int32)])
    owners = jnp.where(
        slot_at < group_sizes[:, None], padded[begin[:, None] + slot_at], -1
    )
    members = lax.dynamic_slice_in_dim(owners, me, 1, axis=0).reshape(GMAX, 1)
    dcos, dsin = tables(prefix_len + cached_len)
    pcos, psin = tables(span_start[0] + jnp.arange(block_rows, dtype=jnp.int32))
    off_arr = jnp.stack(offs).astype(jnp.int32)
    row = jax.ShapeDtypeStruct((dec_count, width), BF16)
    dq, dk, dv = pl.pallas_call(
        functools.partial(dec_qkv_kernel, n, heads),
        out_shape=[row, row, row],
        in_specs=[SM] + [VM] * (n + 3),
        out_specs=[VM] * 3,
        compiler_params=pltpu.CompilerParams(vmem_limit_bytes=BIG),
        name="dec_qkv",
    )(off_arr, *dec_parts, weight, dcos, dsin)
    allq = gather_all(dq, "req", n_req, 1).reshape(n_req * dec_count, width)
    far, near = pl.pallas_call(
        functools.partial(dec_attn_kernel, heads, scale),
        out_shape=[
            jax.ShapeDtypeStruct((GMAX, width + 128), F32),
            jax.ShapeDtypeStruct((dec_count, width + 128), F32),
        ],
        in_specs=[VM] * 9,
        out_specs=[VM] * 2,
        compiler_params=pltpu.CompilerParams(vmem_limit_bytes=BIG),
        name="dec_attn",
    )(allq, members, prefix, dq, dk, dv, pool, page_table, cached_len[:, None])
    got = gather_all(far, "req", n_req, 2).reshape(n_req * GMAX, width + 128)
    dec_ctx = pl.pallas_call(
        functools.partial(merge_kernel, heads),
        out_shape=row,
        in_specs=[SM] + [VM] * 3,
        out_specs=VM,
        compiler_params=pltpu.CompilerParams(vmem_limit_bytes=BIG),
        name="merge",
    )((me * dec_count)[None].astype(jnp.int32), got, owners.reshape(1, -1), near)
    flat_out = out_weight.reshape(width, out_weight.shape[2])
    if n_tp == 2:
        theirs = lax.dynamic_slice_in_dim(flat_out, (1 - side) * share, share, axis=1)
        theirs, pre_parts[1] = lax.optimization_barrier((theirs, pre_parts[1]))
        peer_w = lax.ppermute(theirs, "tp", swap)
        own_w = lax.dynamic_slice_in_dim(flat_out, side * share, share, axis=1)
    chunk = min(128, block_rows)
    scal = jnp.concatenate([off_arr, span_start]).astype(jnp.int32)
    whole = lambda a: pl.BlockSpec(a.shape, lambda i: (0, 0), pipeline_mode=pl.Buffered(1))
    band = lambda w: pl.BlockSpec((chunk, w), lambda i: (i, 0))
    pre_ctx = pl.pallas_call(
        functools.partial(prefill_kernel, n, heads, chunk, scale),
        grid=(block_rows // chunk,),
        out_shape=jax.ShapeDtypeStruct((block_rows, width), BF16),
        in_specs=[SM]
        + [band(p.shape[1]) for p in pre_parts]
        + [whole(weight), band(128), band(128), whole(prefix)],
        out_specs=band(width),
        scratch_shapes=[pltpu.VMEM((block_rows, width), BF16)] * 2,
        compiler_params=pltpu.CompilerParams(vmem_limit_bytes=BIG),
        cost_estimate=pl.CostEstimate(
            flops=int(8e9), bytes_accessed=int(13e6), transcendentals=int(5e6)
        ),
        name="prefill",
    )(scal, *pre_parts, weight, pcos, psin, prefix)
    if n_tp == 2:
        pre_ctxs = [pre_ctx, lax.ppermute(pre_ctx, "tp", swap)]
        dec_ctxs = [dec_ctx, lax.ppermute(dec_ctx, "tp", swap)]
        outs_w, kind = [own_w, peer_w], BF16
    else:
        pre_ctxs, dec_ctxs, outs_w, kind = [pre_ctx], [dec_ctx], [flat_out], F32
    m = len(outs_w)
    span = outs_w[0].shape[1]
    pre_out, dec_out = pl.pallas_call(
        functools.partial(out_kernel, m),
        grid=(block_rows // chunk,),
        out_shape=[
            jax.ShapeDtypeStruct((block_rows, span), kind),
            jax.ShapeDtypeStruct((dec_count, span), kind),
        ],
        in_specs=[band(width)] * m + [whole(d) for d in dec_ctxs] + [whole(w) for w in outs_w],
        out_specs=[band(span), pl.BlockSpec((dec_count, span), lambda i: (0, 0))],
        compiler_params=pltpu.CompilerParams(vmem_limit_bytes=BIG),
        name="out_proj",
    )(*pre_ctxs, *dec_ctxs, *outs_w)
    if n_tp != 2:
        dec_out = lax.psum_scatter(dec_out, "tp", scatter_dimension=1, tiled=True).astype(BF16)
        pre_out = lax.psum_scatter(pre_out, "tp", scatter_dimension=1, tiled=True).astype(BF16)
    return (dec_out, pre_out)


def solution(mesh):
    placed = (
        P("req", "tp"),
        P("req", "tp"),
        P(None, None, "tp", None),
        P("tp", None, None),
        P("req", None, "tp", None, None),
        P("req", None, "tp", None, None),
        P("req", None),
        P("req"),
        P(),
        P(),
        P("req"),
    )
    return jax.shard_map(
        functools.partial(local, mesh.shape["req"], mesh.shape["tp"]),
        mesh=mesh,
        in_specs=placed,
        out_specs=(P("req", "tp"), P("req", "tp")),
        check_vma=False,
    )
```

```python
import functools
import math

import jax
import jax.numpy as jnp
from jax import lax
from jax.experimental import pallas as pl
from jax.experimental.pallas import tpu as pltpu
from jax.sharding import PartitionSpec as P

GMAX = 16
CHUNK = 128
F32, BF16 = jnp.float32, jnp.bfloat16
MESH = pl.DeviceIdType.MESH
VM = pl.BlockSpec(memory_space=pltpu.VMEM)
SM = pl.BlockSpec(memory_space=pltpu.SMEM)
BIG = 56 << 20


def dot(a, b):
    return jnp.dot(a, b, preferred_element_type=F32)


def dot_t(a, b):
    return lax.dot_general(a, b, (((1,), (1,)), ((), ())), preferred_element_type=F32)


def spread_rows(src, dst, tokens, group):
    piece = 16
    while piece * 2 * group <= 256 and piece * 2 <= tokens:
        piece *= 2
    rows = piece * group
    at = lax.broadcasted_iota(jnp.int32, (rows, rows), 0)
    col = lax.broadcasted_iota(jnp.int32, (rows, rows), 1)
    shift = piece.bit_length() - 1
    want = (at & (piece - 1)) * group + lax.shift_right_logical(at, shift)
    pick = jnp.where(col == want, 1.0, 0.0).astype(BF16)
    for k in range(tokens // piece):
        moved = dot(pick, src[k * rows : (k + 1) * rows, :]).astype(BF16)
        for g in range(group):
            dst[k * piece : (k + 1) * piece, g * 128 : (g + 1) * 128] = moved[
                g * piece : (g + 1) * piece, :
            ]


def prep_kernel(groups, tokens, *refs):
    half = len(refs) // 2
    for src, dst, g in zip(refs[:half], refs[half:], groups):
        spread_rows(src, dst, tokens, g)


def prep(arrays, groups, total):
    steps = 16
    tokens = total // steps
    return pl.pallas_call(
        functools.partial(prep_kernel, groups, tokens),
        grid=(steps,),
        out_shape=[jax.ShapeDtypeStruct((total, g * 128), BF16) for g in groups],
        in_specs=[pl.BlockSpec((tokens * g, 128), lambda i: (i, 0)) for g in groups],
        out_specs=[pl.BlockSpec((tokens, g * 128), lambda i: (i, 0)) for g in groups],
        compiler_params=pltpu.CompilerParams(vmem_limit_bytes=BIG),
        cost_estimate=pl.CostEstimate(
            flops=int(2e9), bytes_accessed=int(4 * total * 128 * sum(groups)), transcendentals=0
        ),
        name="prep",
    )(*arrays)


def gather_kernel(axis, count, x_ref, out_ref, send, recv):
    me = lax.axis_index(axis)
    barrier = pltpu.get_barrier_semaphore()

    def greet(k, _):
        pl.semaphore_signal(
            barrier, inc=1, device_id={axis: lax.rem(me + k, count)}, device_id_type=MESH
        )
        return 0

    lax.fori_loop(1, count, greet, 0)
    pl.semaphore_wait(barrier, count - 1)

    def make(k):
        return pltpu.make_async_remote_copy(
            src_ref=x_ref,
            dst_ref=out_ref.at[me],
            send_sem=send.at[k],
            recv_sem=recv.at[k],
            device_id={axis: lax.rem(me + k, count)},
            device_id_type=MESH,
        )

    def go(k, _):
        make(k).start()
        return 0

    lax.fori_loop(1, count, go, 0)
    out_ref[me] = x_ref[...]

    def done(k, _):
        make(k).wait()
        return 0

    lax.fori_loop(1, count, done, 0)


def gather_all(x, axis, count, ident):
    return pl.pallas_call(
        functools.partial(gather_kernel, axis, count),
        out_shape=jax.ShapeDtypeStruct((count,) + x.shape, x.dtype),
        in_specs=[VM],
        out_specs=VM,
        scratch_shapes=[pltpu.SemaphoreType.DMA((count,)), pltpu.SemaphoreType.DMA((count,))],
        compiler_params=pltpu.CompilerParams(collective_id=ident, has_side_effects=True),
        name="gather_all",
    )(x)


def normed_parts(parts):
    wide = [p.astype(F32) for p in parts]
    width = sum(p.shape[1] for p in parts)
    centre = sum(jnp.sum(w, axis=1, keepdims=True) for w in wide) * (1.0 / width)
    moved = [w - centre for w in wide]
    spread = sum(jnp.sum(m * m, axis=1, keepdims=True) for m in moved) * (1.0 / width)
    gain = lax.rsqrt(spread + 1e-05)
    return [(m * gain).astype(BF16) for m in moved]


def qkv_rows(parts, offs, w_ref):
    out = None
    for k, part in enumerate(normed_parts(parts)):
        depth = part.shape[1]
        rows = w_ref[pl.ds(pl.multiple_of(offs[k], 128), depth), :]
        term = dot(part, rows)
        out = term if out is None else out + term
    return out


def turn(y, cos, sin):
    return y * cos + pltpu.roll(y, 64, 1) * sin


def dec_qkv_kernel(n, heads, offs, *refs):
    parts = [r[...] for r in refs[:n]]
    w_ref, cos, sin, q_out, k_out, v_out = refs[n:]
    y = qkv_rows(parts, [offs[k] for k in range(n)], w_ref)
    c, s = cos[...], sin[...]
    for h in range(heads):
        here = slice(h * 128, (h + 1) * 128)
        q_out[:, here] = turn(y[:, h * 128 : (h + 1) * 128], c, s).astype(BF16)
        k_out[:, here] = turn(
            y[:, (heads + h) * 128 : (heads + h + 1) * 128], c, s
        ).astype(BF16)
        v_out[:, here] = y[:, (2 * heads + h) * 128 : (2 * heads + h + 1) * 128].astype(BF16)


def dec_attn_kernel(heads, scale, allq, members, prefix, q, knew, vnew, pool, table, lens, far, near):
    every = allq.shape[0]
    sel = jnp.where(
        members[...] == lax.broadcasted_iota(jnp.int32, (GMAX, every), 1), 1.0, 0.0
    ).astype(BF16)
    chosen = dot(sel, allq[...]).astype(BF16)
    rows = q.shape[0]
    slots = pool.shape[0]
    t = lax.broadcasted_iota(jnp.int32, (rows, slots), 1)
    page, off = lax.shift_right_logical(t, 7), t & 127
    valid = None
    for j in range(table.shape[1]):
        one = (page == table[:, j : j + 1]) & (off + j * 128 < lens[...])
        valid = one if valid is None else valid | one
    lane_f = lax.broadcasted_iota(jnp.int32, (GMAX, 128), 1)
    lane_n = lax.broadcasted_iota(jnp.int32, (rows, 128), 1)
    far_stat = jnp.zeros((GMAX, 128), F32)
    near_stat = jnp.zeros((rows, 128), F32)
    for h in range(heads):
        here = slice(h * 128, (h + 1) * 128)
        kcol = slice(h * 256, h * 256 + 128)
        vcol = slice(h * 256 + 128, h * 256 + 256)
        s = dot_t(chosen[:, here], prefix[:, kcol]) * scale
        m = jnp.max(s, axis=1, keepdims=True)
        w = jnp.exp(s - m)
        far_stat = jnp.where(lane_f == h, m, far_stat)
        far_stat = jnp.where(
            lane_f == heads + h, jnp.sum(w, axis=1, keepdims=True), far_stat
        )
        far[:, here] = dot(w.astype(BF16), prefix[:, vcol])
        qh = q[:, here]
        s = jnp.where(valid, dot_t(qh, pool[:, kcol]) * scale, -1e30)
        own = (
            jnp.sum(qh.astype(F32) * knew[:, here].astype(F32), axis=1, keepdims=True) * scale
        )
        m = jnp.maximum(jnp.max(s, axis=1, keepdims=True), own)
        w = jnp.where(valid, jnp.exp(s - m), 0.0)
        ow = jnp.exp(own - m)
        near_stat = jnp.where(lane_n == h, m, near_stat)
        near_stat = jnp.where(
            lane_n == heads + h, jnp.sum(w, axis=1, keepdims=True) + ow, near_stat
        )
        near[:, here] = dot(w.astype(BF16), pool[:, vcol]) + ow.astype(BF16).astype(
            F32
        ) * vnew[:, here].astype(F32)
    far[:, heads * 128 :] = far_stat
    near[:, heads * 128 :] = near_stat


def merge_kernel(heads, base, got, owners, near, ctx):
    rows = near.shape[0]
    slots = got.shape[0]
    want = base[0] + lax.broadcasted_iota(jnp.int32, (rows, slots), 0)
    pick = jnp.where(owners[...] == want, 1.0, 0.0)
    far = jnp.dot(
        pick, got[...], preferred_element_type=F32, precision=lax.Precision.HIGHEST
    )
    fs, ns = far[:, heads * 128 :], near[:, heads * 128 :]
    for h in range(heads):
        here = slice(h * 128, (h + 1) * 128)
        mp, lp = fs[:, h : h + 1], fs[:, heads + h : heads + h + 1]
        ml, ll = ns[:, h : h + 1], ns[:, heads + h : heads + h + 1]
        top = jnp.maximum(mp, ml)
        a, b = jnp.exp(mp - top), jnp.exp(ml - top)
        ctx[:, here] = (
            (a * far[:, here] + b * near[:, here]) / (a * lp + b * ll)
        ).astype(BF16)


def prefill_kernel(n, heads, rows, scale, scal, *refs):
    parts = [r[...] for r in refs[:n]]
    w_ref, cos, sin, prefix, ctx, kself, vself = refs[n:]
    step = pl.program_id(0)
    start = scal[n]

    @pl.when(step == 0)
    def _():
        kself[...] = jnp.zeros_like(kself)
        vself[...] = jnp.zeros_like(vself)

    y = qkv_rows(parts, [scal[k] for k in range(n)], w_ref)
    c, s = cos[...], sin[...]
    at = pl.ds(pl.multiple_of(step * rows, rows), rows)
    total = kself.shape[0]
    far_len = prefix.shape[0]
    far_bias = jnp.where(
        lax.broadcasted_iota(jnp.int32, (1, far_len), 1) < start, 0.0, -1e30
    )
    near_ok = lax.broadcasted_iota(jnp.int32, (rows, total), 1) <= (
        step * rows + lax.broadcasted_iota(jnp.int32, (rows, total), 0)
    )
    factor = scale * math.log2(math.e)
    for h in range(heads):
        here = slice(h * 128, (h + 1) * 128)
        kcol = slice(h * 256, h * 256 + 128)
        vcol = slice(h * 256 + 128, h * 256 + 256)
        qh = turn(y[:, h * 128 : (h + 1) * 128], c, s).astype(BF16)
        kself[at, here] = turn(
            y[:, (heads + h) * 128 : (heads + h + 1) * 128], c, s
        ).astype(BF16)
        vself[at, here] = y[:, (2 * heads + h) * 128 : (2 * heads + h + 1) * 128].astype(BF16)
        sf = dot_t(qh, prefix[:, kcol]) + far_bias
        sn = jnp.where(near_ok, dot_t(qh, kself[:, here]), -1e30)
        m = jnp.maximum(
            jnp.max(sf, axis=1, keepdims=True), jnp.max(sn, axis=1, keepdims=True)
        )
        wf = jnp.exp2((sf - m) * factor)
        wn = jnp.exp2((sn - m) * factor)
        l = jnp.sum(wf, axis=1, keepdims=True) + jnp.sum(wn, axis=1, keepdims=True)
        o = dot(wf.astype(BF16), prefix[:, vcol]) + dot(wn.astype(BF16), vself[:, here])
        ctx[:, here] = (o / l).astype(BF16)


def out_kernel(n, *refs):
    ctxs, decs, ws = refs[:n], refs[n : 2 * n], refs[2 * n : 3 * n]
    pre_out, dec_out = refs[3 * n :]
    pre_out[...] = sum(dot(c[...], w[...]) for c, w in zip(ctxs, ws)).astype(pre_out.dtype)

    @pl.when(pl.program_id(0) == 0)
    def _():
        dec_out[...] = sum(dot(c[...], w[...]) for c, w in zip(decs, ws)).astype(dec_out.dtype)


def fused_kernel(
    n_req, heads, scale, own_dec, peer_dec, own_pre, peer_pre, w_hbm, prefix_hbm, pool_hbm,
    wout_hbm, dcos, dsin, pcos, psin, sizes, order, table, lens, start,
    dec_out, pre_out,
    w_ref, own_v, peer_v, prefix, pool, wout_own, wout_peer, kself, vself, ctx_own, ctx_peer,
    dctx_own, dctx_peer, myq, allq, qwide, far, farsend, farrecv, near,
    local_sem, q_send, q_recv, f_send, f_recv, t_send, t_recv,
):
    me = lax.axis_index("req")
    side = lax.axis_index("tp")
    other = 1 - side
    rows, share = own_dec.shape
    block = own_pre.shape[0]
    width = heads * 128
    every = n_req * rows
    mine = pl.ds(pl.multiple_of(side * share, 128), share)
    theirs = pl.ds(pl.multiple_of(other * share, 128), share)
    loads = [
        pltpu.make_async_copy(a, b, local_sem.at[k])
        for k, (a, b) in enumerate(
            [
                (w_hbm, w_ref),
                (own_pre, own_v),
                (peer_pre, peer_v),
                (prefix_hbm, prefix),
                (pool_hbm, pool),
                (wout_hbm.at[:, mine], wout_own),
            ]
        )
    ]
    for one in loads:
        one.start()
    barrier = pltpu.get_barrier_semaphore()

    def greet(k, _):
        pl.semaphore_signal(
            barrier, inc=1, device_id={"req": lax.rem(me + k, n_req)}, device_id_type=MESH
        )
        return 0

    lax.fori_loop(1, n_req, greet, 0)
    pl.semaphore_signal(barrier, inc=1, device_id={"tp": other}, device_id_type=MESH)
    pl.semaphore_wait(barrier, n_req)

    def swap(src, dst, k):
        return pltpu.make_async_remote_copy(
            src_ref=src,
            dst_ref=dst,
            send_sem=t_send.at[k],
            recv_sem=t_recv.at[k],
            device_id={"tp": other},
            device_id_type=MESH,
        )

    weight_swap = swap(wout_hbm.at[:, theirs], wout_peer, 0)
    weight_swap.start()

    def q_copy(k):
        return pltpu.make_async_remote_copy(
            src_ref=myq,
            dst_ref=allq.at[me],
            send_sem=q_send.at[k],
            recv_sem=q_recv.at[k],
            device_id={"req": lax.rem(me + k, n_req)},
            device_id_type=MESH,
        )

    def f_copy(k):
        to = lax.rem(me + k, n_req)
        return pltpu.make_async_remote_copy(
            src_ref=farsend.at[to],
            dst_ref=farrecv.at[me],
            send_sem=f_send.at[k],
            recv_sem=f_recv.at[k],
            device_id={"req": to},
            device_id_type=MESH,
        )

    def start_all(make):
        def go(k, _):
            make(k).start()
            return 0

        lax.fori_loop(1, n_req, go, 0)

    def wait_all(make):
        def go(k, _):
            make(k).wait()
            return 0

        lax.fori_loop(1, n_req, go, 0)

    offs = [side * share, other * share]

    loads[0].wait()
    y = qkv_rows([own_dec[...], peer_dec[...]], offs, w_ref)
    c, s = dcos[...], dsin[...]
    dq, dk, dv = [], [], []
    for h in range(heads):
        dq.append(turn(y[:, h * 128 : (h + 1) * 128], c, s).astype(BF16))
        dk.append(
            turn(y[:, (heads + h) * 128 : (heads + h + 1) * 128], c, s).astype(BF16).astype(F32)
        )
        dv.append(
            y[:, (2 * heads + h) * 128 : (2 * heads + h + 1) * 128].astype(BF16).astype(F32)
        )
    for h in range(heads):
        myq[:, h * 128 : (h + 1) * 128] = dq[h]
    start_all(q_copy)
    allq[me] = myq[...]

    lane = lax.broadcasted_iota(jnp.int32, (rows, 128), 1)
    row = lax.broadcasted_iota(jnp.int32, (rows, 128), 0)
    loads[4].wait()
    slots = pool.shape[0]
    t = lax.broadcasted_iota(jnp.int32, (rows, slots), 1)
    page, off = lax.shift_right_logical(t, 7), t & 127
    span = jnp.zeros((rows, 128), jnp.int32)
    for r in range(rows):
        span = jnp.where(row == r, lens[r], span)
    valid = None
    for j in range(table.shape[0]):
        held = jnp.zeros((rows, 128), jnp.int32)
        for r in range(rows):
            held = jnp.where(row == r, table[j, r], held)
        one = (page == held[:, :1]) & (off + j * 128 < span[:, :1])
        valid = one if valid is None else valid | one
    stat = jnp.zeros((rows, 128), F32)
    for h in range(heads):
        here = slice(h * 128, (h + 1) * 128)
        kcol = slice(h * 256, h * 256 + 128)
        vcol = slice(h * 256 + 128, h * 256 + 256)
        sc = jnp.where(valid, dot_t(dq[h], pool[:, kcol]) * scale, -1e30)
        own = jnp.sum(dq[h].astype(F32) * dk[h], axis=1, keepdims=True) * scale
        m = jnp.maximum(jnp.max(sc, axis=1, keepdims=True), own)
        w = jnp.where(valid, jnp.exp(sc - m), 0.0)
        ow = jnp.exp(own - m)
        stat = jnp.where(lane == h, m, stat)
        stat = jnp.where(lane == heads + h, jnp.sum(w, axis=1, keepdims=True) + ow, stat)
        near[:, here] = dot(w.astype(BF16), pool[:, vcol]) + ow.astype(BF16).astype(F32) * dv[h]
    near[:, width:] = stat

    chunk = CHUNK
    far_len = prefix.shape[0]
    bias = jnp.where(
        lax.broadcasted_iota(jnp.int32, (1, far_len), 1) < start[0], 0.0, -1e30
    )
    low = lax.broadcasted_iota(jnp.int32, (chunk, chunk), 1) <= lax.broadcasted_iota(
        jnp.int32, (chunk, chunk), 0
    )
    factor = scale * math.log2(math.e)

    def band(k):
        return slice(k * chunk, (k + 1) * chunk)

    def ctx_swap(k):
        return swap(ctx_own.at[band(k)], ctx_peer.at[band(k)], 2 + k)

    def prefill(k):
        at = band(k)
        y = qkv_rows([own_v[at, :], peer_v[at, :]], offs, w_ref)
        c, s = pcos[at, :], psin[at, :]
        for h in range(heads):
            here = slice(h * 128, (h + 1) * 128)
            kcol = slice(h * 256, h * 256 + 128)
            vcol = slice(h * 256 + 128, h * 256 + 256)
            qh = turn(y[:, h * 128 : (h + 1) * 128], c, s).astype(BF16)
            kh = turn(y[:, (heads + h) * 128 : (heads + h + 1) * 128], c, s).astype(BF16)
            vh = y[:, (2 * heads + h) * 128 : (2 * heads + h + 1) * 128].astype(BF16)
            kself[at, here] = kh
            vself[at, here] = vh
            pieces = [(dot_t(qh, prefix[:, kcol]) + bias, prefix, vcol, slice(0, far_len))]
            if k:
                back = slice(0, k * chunk)
                pieces.append((dot_t(qh, kself[back, here]), vself, here, back))
            tip = jnp.where(low, dot_t(qh, kh), -1e30)
            m = jnp.max(tip, axis=1, keepdims=True)
            for sc, _, _, _ in pieces:
                m = jnp.maximum(m, jnp.max(sc, axis=1, keepdims=True))
            w = jnp.exp2((tip - m) * factor)
            l = jnp.sum(w, axis=1, keepdims=True)
            o = dot(w.astype(BF16), vh)
            for sc, ref, cols, part in pieces:
                w = jnp.exp2((sc - m) * factor)
                l = l + jnp.sum(w, axis=1, keepdims=True)
                o = o + dot(w.astype(BF16), ref[part, cols])
            ctx_own[at, here] = (o / l).astype(BF16)
        ctx_swap(k).start()

    loads[1].wait()
    loads[2].wait()
    loads[3].wait()
    prefill(0)

    wait_all(q_copy)
    for g in range(n_req):
        qwide[g * rows : (g + 1) * rows, :] = allq[g].astype(F32)
    begin, size = jnp.int32(0), jnp.int32(0)
    for g in range(n_req):
        begin = begin + jnp.where(g < me, sizes[g], 0)
        size = size + jnp.where(g == me, sizes[g], 0)
    slot = lax.broadcasted_iota(jnp.int32, (GMAX, every), 0)
    rank = lax.broadcasted_iota(jnp.int32, (GMAX, every), 1)
    held = jnp.where((rank == begin + slot) & (slot < size), 1.0, 0.0).astype(BF16)
    named = jnp.where(
        order[...] == lax.broadcasted_iota(jnp.int32, (every, every), 0), 1.0, 0.0
    ).astype(BF16)
    pick = dot_t(held, named).astype(BF16)
    back = dot_t(named, held)
    chosen = dot(pick, qwide[...].astype(BF16)).astype(BF16)
    lane = lax.broadcasted_iota(jnp.int32, (GMAX, 128), 1)
    stat = jnp.zeros((GMAX, 128), F32)
    for h in range(heads):
        here = slice(h * 128, (h + 1) * 128)
        kcol = slice(h * 256, h * 256 + 128)
        vcol = slice(h * 256 + 128, h * 256 + 256)
        sc = dot_t(chosen[:, here], prefix[:, kcol]) * scale
        m = jnp.max(sc, axis=1, keepdims=True)
        w = jnp.exp(sc - m)
        stat = jnp.where(lane == h, m, stat)
        stat = jnp.where(lane == heads + h, jnp.sum(w, axis=1, keepdims=True), stat)
        far[:, here] = dot(w.astype(BF16), prefix[:, vcol])
    far[:, width:] = stat
    spread = jnp.dot(
        back, far[...], preferred_element_type=F32, precision=lax.Precision.HIGHEST
    )
    for g in range(n_req):
        farsend[g] = spread[g * rows : (g + 1) * rows, :]
    start_all(f_copy)
    farrecv[me] = farsend[me]

    count = block // chunk
    for k in range(1, count - 1):
        prefill(k)

    wait_all(f_copy)
    got = farrecv[0]
    for g in range(1, n_req):
        got = got + farrecv[g]
    for h in range(heads):
        here = slice(h * 128, (h + 1) * 128)
        mp, lp = got[:, width + h : width + h + 1], got[:, width + heads + h : width + heads + h + 1]
        ml = near[:, width + h : width + h + 1]
        ll = near[:, width + heads + h : width + heads + h + 1]
        top = jnp.maximum(mp, ml)
        a, b = jnp.exp(mp - top), jnp.exp(ml - top)
        dctx_own[:, here] = ((a * got[:, here] + b * near[:, here]) / (a * lp + b * ll)).astype(BF16)
    dec_swap = swap(dctx_own, dctx_peer, 1)
    dec_swap.start()
    prefill(count - 1)

    loads[5].wait()
    weight_swap.wait()
    dec_swap.wait()
    dec_out[...] = (
        dot(dctx_own[...], wout_own[...]) + dot(dctx_peer[...], wout_peer[...])
    ).astype(BF16)
    for k in range(count):
        ctx_swap(k).wait()
        at = band(k)
        pre_out[at, :] = (
            dot(ctx_own[at, :], wout_own[...]) + dot(ctx_peer[at, :], wout_peer[...])
        ).astype(BF16)


def places_tables(places):
    lane = jnp.arange(128, dtype=jnp.int32)
    inverse = 10000.0 ** (-((lane & 63).astype(F32) / 64))
    angles = places.astype(F32)[:, None] * inverse[None, :]
    return jnp.cos(angles), jnp.sin(angles) * jnp.where(lane < 64, -1.0, 1.0)[None, :]


def fused(
    n_req, own_dec, peer_dec, own_pre, peer_pre, weight, prefix, pool, flat_out,
    group_sizes, member_order, page_table, cached_len, span_start,
):
    rows, share = own_dec.shape
    block = own_pre.shape[0]
    width = flat_out.shape[0]
    heads = width // 128
    every = n_req * rows
    dcos, dsin = places_tables(prefix.shape[0] + cached_len)
    pcos, psin = places_tables(span_start[0] + jnp.arange(block, dtype=jnp.int32))
    anyw = pl.BlockSpec(memory_space=pl.ANY)
    dma = pltpu.SemaphoreType.DMA
    count = block // CHUNK
    return pl.pallas_call(
        functools.partial(fused_kernel, n_req, heads, 128 ** (-0.5)),
        out_shape=[
            jax.ShapeDtypeStruct((rows, share), BF16),
            jax.ShapeDtypeStruct((block, share), BF16),
        ],
        in_specs=[VM, VM] + [anyw] * 6 + [VM] * 4 + [SM, VM, SM, SM, SM],
        out_specs=[VM, VM],
        scratch_shapes=[
            pltpu.VMEM(weight.shape, BF16),
            pltpu.VMEM((block, share), BF16),
            pltpu.VMEM((block, share), BF16),
            pltpu.VMEM(prefix.shape, BF16),
            pltpu.VMEM(pool.shape, BF16),
            pltpu.VMEM((width, share), BF16),
            pltpu.VMEM((width, share), BF16),
            pltpu.VMEM((block, width), BF16),
            pltpu.VMEM((block, width), BF16),
            pltpu.VMEM((block, width), BF16),
            pltpu.VMEM((block, width), BF16),
            pltpu.VMEM((rows, width), BF16),
            pltpu.VMEM((rows, width), BF16),
            pltpu.VMEM((rows, width), BF16),
            pltpu.VMEM((n_req, rows, width), BF16),
            pltpu.VMEM((every, width), F32),
            pltpu.VMEM((GMAX, width + 128), F32),
            pltpu.VMEM((n_req, rows, width + 128), F32),
            pltpu.VMEM((n_req, rows, width + 128), F32),
            pltpu.VMEM((rows, width + 128), F32),
            dma((6,)),
            dma((n_req,)),
            dma((n_req,)),
            dma((n_req,)),
            dma((n_req,)),
            dma((2 + count,)),
            dma((2 + count,)),
        ],
        compiler_params=pltpu.CompilerParams(
            collective_id=3, has_side_effects=True, vmem_limit_bytes=BIG
        ),
        name="fused",
    )(
        own_dec, peer_dec, own_pre, peer_pre, weight, prefix, pool, flat_out,
        dcos, dsin, pcos, psin, group_sizes, member_order[None, :], page_table.T, cached_len,
        span_start,
    )


def tables(places):
    inverse = 10000.0 ** (-(jnp.arange(64, dtype=F32) / 64))
    angles = places.astype(F32)[:, None] * inverse[None, :]
    c, s = jnp.cos(angles), jnp.sin(angles)
    return jnp.concatenate([c, c], axis=1), jnp.concatenate([-s, s], axis=1)


def local(
    n_req,
    n_tp,
    decode_tokens,
    prefill_tokens,
    qkv_weight,
    out_weight,
    prefix_cache,
    page_pool,
    page_table,
    cached_len,
    group_sizes,
    member_order,
    span_start,
):
    heads = qkv_weight.shape[2]
    width = heads * 128
    features = qkv_weight.shape[0]
    scale = 128 ** (-0.5)
    prefix_len = prefix_cache.shape[1]
    block_rows, share = prefill_tokens.shape
    dec_count = decode_tokens.shape[0]
    me = lax.axis_index("req")
    side = lax.axis_index("tp")
    swap = [(0, 1), (1, 0)]
    if n_tp == 2:
        dec_parts = [decode_tokens, lax.ppermute(decode_tokens, "tp", swap)]
        pre_parts = [prefill_tokens, lax.ppermute(prefill_tokens, "tp", swap)]
        offs = [side * share, (1 - side) * share]
    else:
        dec_parts = [lax.all_gather(decode_tokens, "tp", axis=1, tiled=True)]
        pre_parts = [lax.all_gather(prefill_tokens, "tp", axis=1, tiled=True)]
        offs = [jnp.int32(0)]
    n = len(offs)
    slots = page_pool.shape[0] * page_pool.shape[1]
    weight, prefix, pool = prep(
        [
            qkv_weight.reshape(-1, 128),
            prefix_cache.reshape(-1, 128),
            page_pool.reshape(-1, 128),
        ],
        [3 * heads, 2 * heads, 2 * heads],
        features,
    ) if features == prefix_len == slots else (
        prep([qkv_weight.reshape(-1, 128)], [3 * heads], features)
        + prep([prefix_cache.reshape(-1, 128)], [2 * heads], prefix_len)
        + prep([page_pool.reshape(-1, 128)], [2 * heads], slots)
    )
    if n_tp == 2 and block_rows % CHUNK == 0 and block_rows > CHUNK:
        dec_out, pre_out = fused(
            n_req, *dec_parts, *pre_parts, weight, prefix, pool,
            out_weight.reshape(width, out_weight.shape[2]),
            group_sizes, member_order, page_table, cached_len, span_start,
        )
        return (dec_out, pre_out)
    begin = jnp.cumsum(group_sizes) - group_sizes
    slot_at = jnp.arange(GMAX, dtype=jnp.int32)[None, :]
    padded = jnp.concatenate([member_order, jnp.zeros((GMAX,), jnp.int32)])
    owners = jnp.where(
        slot_at < group_sizes[:, None], padded[begin[:, None] + slot_at], -1
    )
    members = lax.dynamic_slice_in_dim(owners, me, 1, axis=0).reshape(GMAX, 1)
    dcos, dsin = tables(prefix_len + cached_len)
    pcos, psin = tables(span_start[0] + jnp.arange(block_rows, dtype=jnp.int32))
    off_arr = jnp.stack(offs).astype(jnp.int32)
    row = jax.ShapeDtypeStruct((dec_count, width), BF16)
    dq, dk, dv = pl.pallas_call(
        functools.partial(dec_qkv_kernel, n, heads),
        out_shape=[row, row, row],
        in_specs=[SM] + [VM] * (n + 3),
        out_specs=[VM] * 3,
        compiler_params=pltpu.CompilerParams(vmem_limit_bytes=BIG),
        name="dec_qkv",
    )(off_arr, *dec_parts, weight, dcos, dsin)
    allq = gather_all(dq, "req", n_req, 1).reshape(n_req * dec_count, width)
    far, near = pl.pallas_call(
        functools.partial(dec_attn_kernel, heads, scale),
        out_shape=[
            jax.ShapeDtypeStruct((GMAX, width + 128), F32),
            jax.ShapeDtypeStruct((dec_count, width + 128), F32),
        ],
        in_specs=[VM] * 9,
        out_specs=[VM] * 2,
        compiler_params=pltpu.CompilerParams(vmem_limit_bytes=BIG),
        name="dec_attn",
    )(allq, members, prefix, dq, dk, dv, pool, page_table, cached_len[:, None])
    got = gather_all(far, "req", n_req, 2).reshape(n_req * GMAX, width + 128)
    dec_ctx = pl.pallas_call(
        functools.partial(merge_kernel, heads),
        out_shape=row,
        in_specs=[SM] + [VM] * 3,
        out_specs=VM,
        compiler_params=pltpu.CompilerParams(vmem_limit_bytes=BIG),
        name="merge",
    )((me * dec_count)[None].astype(jnp.int32), got, owners.reshape(1, -1), near)
    flat_out = out_weight.reshape(width, out_weight.shape[2])
    if n_tp == 2:
        theirs = lax.dynamic_slice_in_dim(flat_out, (1 - side) * share, share, axis=1)
        theirs, pre_parts[1] = lax.optimization_barrier((theirs, pre_parts[1]))
        peer_w = lax.ppermute(theirs, "tp", swap)
        own_w = lax.dynamic_slice_in_dim(flat_out, side * share, share, axis=1)
    chunk = min(128, block_rows)
    scal = jnp.concatenate([off_arr, span_start]).astype(jnp.int32)
    whole = lambda a: pl.BlockSpec(a.shape, lambda i: (0, 0), pipeline_mode=pl.Buffered(1))
    band = lambda w: pl.BlockSpec((chunk, w), lambda i: (i, 0))
    pre_ctx = pl.pallas_call(
        functools.partial(prefill_kernel, n, heads, chunk, scale),
        grid=(block_rows // chunk,),
        out_shape=jax.ShapeDtypeStruct((block_rows, width), BF16),
        in_specs=[SM]
        + [band(p.shape[1]) for p in pre_parts]
        + [whole(weight), band(128), band(128), whole(prefix)],
        out_specs=band(width),
        scratch_shapes=[pltpu.VMEM((block_rows, width), BF16)] * 2,
        compiler_params=pltpu.CompilerParams(vmem_limit_bytes=BIG),
        cost_estimate=pl.CostEstimate(
            flops=int(8e9), bytes_accessed=int(13e6), transcendentals=int(5e6)
        ),
        name="prefill",
    )(scal, *pre_parts, weight, pcos, psin, prefix)
    if n_tp == 2:
        pre_ctxs = [pre_ctx, lax.ppermute(pre_ctx, "tp", swap)]
        dec_ctxs = [dec_ctx, lax.ppermute(dec_ctx, "tp", swap)]
        outs_w, kind = [own_w, peer_w], BF16
    else:
        pre_ctxs, dec_ctxs, outs_w, kind = [pre_ctx], [dec_ctx], [flat_out], F32
    m = len(outs_w)
    span = outs_w[0].shape[1]
    pre_out, dec_out = pl.pallas_call(
        functools.partial(out_kernel, m),
        grid=(block_rows // chunk,),
        out_shape=[
            jax.ShapeDtypeStruct((block_rows, span), kind),
            jax.ShapeDtypeStruct((dec_count, span), kind),
        ],
        in_specs=[band(width)] * m + [whole(d) for d in dec_ctxs] + [whole(w) for w in outs_w],
        out_specs=[band(span), pl.BlockSpec((dec_count, span), lambda i: (0, 0))],
        compiler_params=pltpu.CompilerParams(vmem_limit_bytes=BIG),
        name="out_proj",
    )(*pre_ctxs, *dec_ctxs, *outs_w)
    if n_tp != 2:
        dec_out = lax.psum_scatter(dec_out, "tp", scatter_dimension=1, tiled=True).astype(BF16)
        pre_out = lax.psum_scatter(pre_out, "tp", scatter_dimension=1, tiled=True).astype(BF16)
    return (dec_out, pre_out)


def solution(mesh):
    placed = (
        P("req", "tp"),
        P("req", "tp"),
        P(None, None, "tp", None),
        P("tp", None, None),
        P("req", None, "tp", None, None),
        P("req", None, "tp", None, None),
        P("req", None),
        P("req"),
        P(),
        P(),
        P("req"),
    )
    return jax.shard_map(
        functools.partial(local, mesh.shape["req"], mesh.shape["tp"]),
        mesh=mesh,
        in_specs=placed,
        out_specs=(P("req", "tp"), P("req", "tp")),
        check_vma=False,
    )
```

```python
import functools
import math

import jax
import jax.numpy as jnp
from jax import lax
from jax.experimental import pallas as pl
from jax.experimental.pallas import tpu as pltpu
from jax.sharding import PartitionSpec as P

GMAX = 16
CHUNK = 128
F32, BF16 = jnp.float32, jnp.bfloat16
MESH = pl.DeviceIdType.MESH
VM = pl.BlockSpec(memory_space=pltpu.VMEM)
SM = pl.BlockSpec(memory_space=pltpu.SMEM)
BIG = 56 << 20


def dot(a, b):
    return jnp.dot(a, b, preferred_element_type=F32)


def dot_t(a, b):
    return lax.dot_general(a, b, (((1,), (1,)), ((), ())), preferred_element_type=F32)


def spread_rows(src, dst, tokens, group):
    piece = 16
    while piece * 2 * group <= 256 and piece * 2 <= tokens:
        piece *= 2
    rows = piece * group
    at = lax.broadcasted_iota(jnp.int32, (rows, rows), 0)
    col = lax.broadcasted_iota(jnp.int32, (rows, rows), 1)
    shift = piece.bit_length() - 1
    want = (at & (piece - 1)) * group + lax.shift_right_logical(at, shift)
    pick = jnp.where(col == want, 1.0, 0.0).astype(BF16)
    for k in range(tokens // piece):
        moved = dot(pick, src[k * rows : (k + 1) * rows, :]).astype(BF16)
        for g in range(group):
            dst[k * piece : (k + 1) * piece, g * 128 : (g + 1) * 128] = moved[
                g * piece : (g + 1) * piece, :
            ]


def prep_kernel(groups, tokens, *refs):
    half = len(refs) // 2
    for src, dst, g in zip(refs[:half], refs[half:], groups):
        spread_rows(src, dst, tokens, g)


def prep(arrays, groups, total):
    steps = 16
    tokens = total // steps
    return pl.pallas_call(
        functools.partial(prep_kernel, groups, tokens),
        grid=(steps,),
        out_shape=[jax.ShapeDtypeStruct((total, g * 128), BF16) for g in groups],
        in_specs=[pl.BlockSpec((tokens * g, 128), lambda i: (i, 0)) for g in groups],
        out_specs=[pl.BlockSpec((tokens, g * 128), lambda i: (i, 0)) for g in groups],
        compiler_params=pltpu.CompilerParams(vmem_limit_bytes=BIG),
        cost_estimate=pl.CostEstimate(
            flops=int(2e9), bytes_accessed=int(4 * total * 128 * sum(groups)), transcendentals=0
        ),
        name="prep",
    )(*arrays)


def gather_kernel(axis, count, x_ref, out_ref, send, recv):
    me = lax.axis_index(axis)
    barrier = pltpu.get_barrier_semaphore()

    def greet(k, _):
        pl.semaphore_signal(
            barrier, inc=1, device_id={axis: lax.rem(me + k, count)}, device_id_type=MESH
        )
        return 0

    lax.fori_loop(1, count, greet, 0)
    pl.semaphore_wait(barrier, count - 1)

    def make(k):
        return pltpu.make_async_remote_copy(
            src_ref=x_ref,
            dst_ref=out_ref.at[me],
            send_sem=send.at[k],
            recv_sem=recv.at[k],
            device_id={axis: lax.rem(me + k, count)},
            device_id_type=MESH,
        )

    def go(k, _):
        make(k).start()
        return 0

    lax.fori_loop(1, count, go, 0)
    out_ref[me] = x_ref[...]

    def done(k, _):
        make(k).wait()
        return 0

    lax.fori_loop(1, count, done, 0)


def gather_all(x, axis, count, ident):
    return pl.pallas_call(
        functools.partial(gather_kernel, axis, count),
        out_shape=jax.ShapeDtypeStruct((count,) + x.shape, x.dtype),
        in_specs=[VM],
        out_specs=VM,
        scratch_shapes=[pltpu.SemaphoreType.DMA((count,)), pltpu.SemaphoreType.DMA((count,))],
        compiler_params=pltpu.CompilerParams(collective_id=ident, has_side_effects=True),
        name="gather_all",
    )(x)


def normed_parts(parts):
    wide = [p.astype(F32) for p in parts]
    width = sum(p.shape[1] for p in parts)
    centre = sum(jnp.sum(w, axis=1, keepdims=True) for w in wide) * (1.0 / width)
    moved = [w - centre for w in wide]
    spread = sum(jnp.sum(m * m, axis=1, keepdims=True) for m in moved) * (1.0 / width)
    gain = lax.rsqrt(spread + 1e-05)
    return [(m * gain).astype(BF16) for m in moved]


def qkv_rows(parts, offs, w_ref):
    out = None
    for k, part in enumerate(normed_parts(parts)):
        depth = part.shape[1]
        rows = w_ref[pl.ds(pl.multiple_of(offs[k], 128), depth), :]
        term = dot(part, rows)
        out = term if out is None else out + term
    return out


def turn(y, cos, sin):
    return y * cos + pltpu.roll(y, 64, 1) * sin


def dec_qkv_kernel(n, heads, offs, *refs):
    parts = [r[...] for r in refs[:n]]
    w_ref, cos, sin, q_out, k_out, v_out = refs[n:]
    y = qkv_rows(parts, [offs[k] for k in range(n)], w_ref)
    c, s = cos[...], sin[...]
    for h in range(heads):
        here = slice(h * 128, (h + 1) * 128)
        q_out[:, here] = turn(y[:, h * 128 : (h + 1) * 128], c, s).astype(BF16)
        k_out[:, here] = turn(
            y[:, (heads + h) * 128 : (heads + h + 1) * 128], c, s
        ).astype(BF16)
        v_out[:, here] = y[:, (2 * heads + h) * 128 : (2 * heads + h + 1) * 128].astype(BF16)


def dec_attn_kernel(heads, scale, allq, members, prefix, q, knew, vnew, pool, table, lens, far, near):
    every = allq.shape[0]
    sel = jnp.where(
        members[...] == lax.broadcasted_iota(jnp.int32, (GMAX, every), 1), 1.0, 0.0
    ).astype(BF16)
    chosen = dot(sel, allq[...]).astype(BF16)
    rows = q.shape[0]
    slots = pool.shape[0]
    t = lax.broadcasted_iota(jnp.int32, (rows, slots), 1)
    page, off = lax.shift_right_logical(t, 7), t & 127
    valid = None
    for j in range(table.shape[1]):
        one = (page == table[:, j : j + 1]) & (off + j * 128 < lens[...])
        valid = one if valid is None else valid | one
    lane_f = lax.broadcasted_iota(jnp.int32, (GMAX, 128), 1)
    lane_n = lax.broadcasted_iota(jnp.int32, (rows, 128), 1)
    far_stat = jnp.zeros((GMAX, 128), F32)
    near_stat = jnp.zeros((rows, 128), F32)
    for h in range(heads):
        here = slice(h * 128, (h + 1) * 128)
        kcol = slice(h * 256, h * 256 + 128)
        vcol = slice(h * 256 + 128, h * 256 + 256)
        s = dot_t(chosen[:, here], prefix[:, kcol]) * scale
        m = jnp.max(s, axis=1, keepdims=True)
        w = jnp.exp(s - m)
        far_stat = jnp.where(lane_f == h, m, far_stat)
        far_stat = jnp.where(
            lane_f == heads + h, jnp.sum(w, axis=1, keepdims=True), far_stat
        )
        far[:, here] = dot(w.astype(BF16), prefix[:, vcol])
        qh = q[:, here]
        s = jnp.where(valid, dot_t(qh, pool[:, kcol]) * scale, -1e30)
        own = (
            jnp.sum(qh.astype(F32) * knew[:, here].astype(F32), axis=1, keepdims=True) * scale
        )
        m = jnp.maximum(jnp.max(s, axis=1, keepdims=True), own)
        w = jnp.where(valid, jnp.exp(s - m), 0.0)
        ow = jnp.exp(own - m)
        near_stat = jnp.where(lane_n == h, m, near_stat)
        near_stat = jnp.where(
            lane_n == heads + h, jnp.sum(w, axis=1, keepdims=True) + ow, near_stat
        )
        near[:, here] = dot(w.astype(BF16), pool[:, vcol]) + ow.astype(BF16).astype(
            F32
        ) * vnew[:, here].astype(F32)
    far[:, heads * 128 :] = far_stat
    near[:, heads * 128 :] = near_stat


def merge_kernel(heads, base, got, owners, near, ctx):
    rows = near.shape[0]
    slots = got.shape[0]
    want = base[0] + lax.broadcasted_iota(jnp.int32, (rows, slots), 0)
    pick = jnp.where(owners[...] == want, 1.0, 0.0)
    far = jnp.dot(
        pick, got[...], preferred_element_type=F32, precision=lax.Precision.HIGHEST
    )
    fs, ns = far[:, heads * 128 :], near[:, heads * 128 :]
    for h in range(heads):
        here = slice(h * 128, (h + 1) * 128)
        mp, lp = fs[:, h : h + 1], fs[:, heads + h : heads + h + 1]
        ml, ll = ns[:, h : h + 1], ns[:, heads + h : heads + h + 1]
        top = jnp.maximum(mp, ml)
        a, b = jnp.exp(mp - top), jnp.exp(ml - top)
        ctx[:, here] = (
            (a * far[:, here] + b * near[:, here]) / (a * lp + b * ll)
        ).astype(BF16)


def prefill_kernel(n, heads, rows, scale, scal, *refs):
    parts = [r[...] for r in refs[:n]]
    w_ref, cos, sin, prefix, ctx, kself, vself = refs[n:]
    step = pl.program_id(0)
    start = scal[n]

    @pl.when(step == 0)
    def _():
        kself[...] = jnp.zeros_like(kself)
        vself[...] = jnp.zeros_like(vself)

    y = qkv_rows(parts, [scal[k] for k in range(n)], w_ref)
    c, s = cos[...], sin[...]
    at = pl.ds(pl.multiple_of(step * rows, rows), rows)
    total = kself.shape[0]
    far_len = prefix.shape[0]
    far_bias = jnp.where(
        lax.broadcasted_iota(jnp.int32, (1, far_len), 1) < start, 0.0, -1e30
    )
    near_ok = lax.broadcasted_iota(jnp.int32, (rows, total), 1) <= (
        step * rows + lax.broadcasted_iota(jnp.int32, (rows, total), 0)
    )
    factor = scale * math.log2(math.e)
    for h in range(heads):
        here = slice(h * 128, (h + 1) * 128)
        kcol = slice(h * 256, h * 256 + 128)
        vcol = slice(h * 256 + 128, h * 256 + 256)
        qh = turn(y[:, h * 128 : (h + 1) * 128], c, s).astype(BF16)
        kself[at, here] = turn(
            y[:, (heads + h) * 128 : (heads + h + 1) * 128], c, s
        ).astype(BF16)
        vself[at, here] = y[:, (2 * heads + h) * 128 : (2 * heads + h + 1) * 128].astype(BF16)
        sf = dot_t(qh, prefix[:, kcol]) + far_bias
        sn = jnp.where(near_ok, dot_t(qh, kself[:, here]), -1e30)
        m = jnp.maximum(
            jnp.max(sf, axis=1, keepdims=True), jnp.max(sn, axis=1, keepdims=True)
        )
        wf = jnp.exp2((sf - m) * factor)
        wn = jnp.exp2((sn - m) * factor)
        l = jnp.sum(wf, axis=1, keepdims=True) + jnp.sum(wn, axis=1, keepdims=True)
        o = dot(wf.astype(BF16), prefix[:, vcol]) + dot(wn.astype(BF16), vself[:, here])
        ctx[:, here] = (o / l).astype(BF16)


def out_kernel(n, *refs):
    ctxs, decs, ws = refs[:n], refs[n : 2 * n], refs[2 * n : 3 * n]
    pre_out, dec_out = refs[3 * n :]
    pre_out[...] = sum(dot(c[...], w[...]) for c, w in zip(ctxs, ws)).astype(pre_out.dtype)

    @pl.when(pl.program_id(0) == 0)
    def _():
        dec_out[...] = sum(dot(c[...], w[...]) for c, w in zip(decs, ws)).astype(dec_out.dtype)


def fused_kernel(
    n_req, heads, scale, own_dec, own_pre, peer_pre, w_hbm, prefix_hbm, pool_hbm,
    wout_hbm, dcos, dsin, pcos, psin, sizes, order, table, lens, start,
    dec_out, pre_out,
    peer_dec, w_ref, own_v, peer_v, prefix, pool, wout_own, wout_peer, kself, vself, ctx_own, ctx_peer,
    dctx_own, dctx_peer, myq, allq, qwide, far, farsend, farrecv, near,
    local_sem, q_send, q_recv, f_send, f_recv, t_send, t_recv,
):
    me = lax.axis_index("req")
    side = lax.axis_index("tp")
    other = 1 - side
    rows, share = own_dec.shape
    block = own_pre.shape[0]
    width = heads * 128
    every = n_req * rows
    mine = pl.ds(pl.multiple_of(side * share, 128), share)
    theirs = pl.ds(pl.multiple_of(other * share, 128), share)
    loads = [
        pltpu.make_async_copy(a, b, local_sem.at[k])
        for k, (a, b) in enumerate(
            [
                (w_hbm, w_ref),
                (own_pre, own_v),
                (peer_pre, peer_v.at[: peer_pre.shape[0]]),
                (prefix_hbm, prefix),
                (pool_hbm, pool),
                (wout_hbm.at[:, mine], wout_own),
            ]
        )
    ]
    for one in loads:
        one.start()
    barrier = pltpu.get_barrier_semaphore()

    def greet(k, _):
        pl.semaphore_signal(
            barrier, inc=1, device_id={"req": lax.rem(me + k, n_req)}, device_id_type=MESH
        )
        return 0

    lax.fori_loop(1, n_req, greet, 0)
    pl.semaphore_signal(barrier, inc=1, device_id={"tp": other}, device_id_type=MESH)
    pl.semaphore_wait(barrier, n_req)

    def swap(src, dst, k):
        return pltpu.make_async_remote_copy(
            src_ref=src,
            dst_ref=dst,
            send_sem=t_send.at[k],
            recv_sem=t_recv.at[k],
            device_id={"tp": other},
            device_id_type=MESH,
        )

    count = block // CHUNK
    dec_tokens_swap = swap(own_dec, peer_dec, 2 + count)
    dec_tokens_swap.start()
    last = slice(peer_pre.shape[0], block)
    last_swap = swap(own_pre.at[last], peer_v.at[last], 3 + count)
    last_swap.start()
    weight_swap = swap(wout_hbm.at[:, theirs], wout_peer, 0)
    weight_swap.start()

    def q_copy(k):
        return pltpu.make_async_remote_copy(
            src_ref=myq,
            dst_ref=allq.at[me],
            send_sem=q_send.at[k],
            recv_sem=q_recv.at[k],
            device_id={"req": lax.rem(me + k, n_req)},
            device_id_type=MESH,
        )

    def f_copy(k):
        to = lax.rem(me + k, n_req)
        return pltpu.make_async_remote_copy(
            src_ref=farsend.at[to],
            dst_ref=farrecv.at[me],
            send_sem=f_send.at[k],
            recv_sem=f_recv.at[k],
            device_id={"req": to},
            device_id_type=MESH,
        )

    def start_all(make):
        def go(k, _):
            make(k).start()
            return 0

        lax.fori_loop(1, n_req, go, 0)

    def wait_all(make):
        def go(k, _):
            make(k).wait()
            return 0

        lax.fori_loop(1, n_req, go, 0)

    offs = [side * share, other * share]

    loads[0].wait()
    dec_tokens_swap.wait()
    y = qkv_rows([own_dec[...], peer_dec[...]], offs, w_ref)
    c, s = dcos[...], dsin[...]
    dq, dk, dv = [], [], []
    for h in range(heads):
        dq.append(turn(y[:, h * 128 : (h + 1) * 128], c, s).astype(BF16))
        dk.append(
            turn(y[:, (heads + h) * 128 : (heads + h + 1) * 128], c, s).astype(BF16).astype(F32)
        )
        dv.append(
            y[:, (2 * heads + h) * 128 : (2 * heads + h + 1) * 128].astype(BF16).astype(F32)
        )
    for h in range(heads):
        myq[:, h * 128 : (h + 1) * 128] = dq[h]
    start_all(q_copy)
    allq[me] = myq[...]

    lane = lax.broadcasted_iota(jnp.int32, (rows, 128), 1)
    row = lax.broadcasted_iota(jnp.int32, (rows, 128), 0)
    loads[4].wait()
    slots = pool.shape[0]
    t = lax.broadcasted_iota(jnp.int32, (rows, slots), 1)
    page, off = lax.shift_right_logical(t, 7), t & 127
    span = jnp.zeros((rows, 128), jnp.int32)
    for r in range(rows):
        span = jnp.where(row == r, lens[r], span)
    valid = None
    for j in range(table.shape[0]):
        held = jnp.zeros((rows, 128), jnp.int32)
        for r in range(rows):
            held = jnp.where(row == r, table[j, r], held)
        one = (page == held[:, :1]) & (off + j * 128 < span[:, :1])
        valid = one if valid is None else valid | one
    stat = jnp.zeros((rows, 128), F32)
    for h in range(heads):
        here = slice(h * 128, (h + 1) * 128)
        kcol = slice(h * 256, h * 256 + 128)
        vcol = slice(h * 256 + 128, h * 256 + 256)
        sc = jnp.where(valid, dot_t(dq[h], pool[:, kcol]) * scale, -1e30)
        own = jnp.sum(dq[h].astype(F32) * dk[h], axis=1, keepdims=True) * scale
        m = jnp.maximum(jnp.max(sc, axis=1, keepdims=True), own)
        w = jnp.where(valid, jnp.exp(sc - m), 0.0)
        ow = jnp.exp(own - m)
        stat = jnp.where(lane == h, m, stat)
        stat = jnp.where(lane == heads + h, jnp.sum(w, axis=1, keepdims=True) + ow, stat)
        near[:, here] = dot(w.astype(BF16), pool[:, vcol]) + ow.astype(BF16).astype(F32) * dv[h]
    near[:, width:] = stat

    chunk = CHUNK
    far_len = prefix.shape[0]
    bias = jnp.where(
        lax.broadcasted_iota(jnp.int32, (1, far_len), 1) < start[0], 0.0, -1e30
    )
    low = lax.broadcasted_iota(jnp.int32, (chunk, chunk), 1) <= lax.broadcasted_iota(
        jnp.int32, (chunk, chunk), 0
    )
    factor = scale * math.log2(math.e)

    def band(k):
        return slice(k * chunk, (k + 1) * chunk)

    def ctx_swap(k):
        return swap(ctx_own.at[band(k)], ctx_peer.at[band(k)], 2 + k)

    def prefill(k):
        at = band(k)
        y = qkv_rows([own_v[at, :], peer_v[at, :]], offs, w_ref)
        c, s = pcos[at, :], psin[at, :]
        for h in range(heads):
            here = slice(h * 128, (h + 1) * 128)
            kcol = slice(h * 256, h * 256 + 128)
            vcol = slice(h * 256 + 128, h * 256 + 256)
            qh = turn(y[:, h * 128 : (h + 1) * 128], c, s).astype(BF16)
            kh = turn(y[:, (heads + h) * 128 : (heads + h + 1) * 128], c, s).astype(BF16)
            vh = y[:, (2 * heads + h) * 128 : (2 * heads + h + 1) * 128].astype(BF16)
            kself[at, here] = kh
            vself[at, here] = vh
            pieces = [(dot_t(qh, prefix[:, kcol]) + bias, prefix, vcol, slice(0, far_len))]
            if k:
                back = slice(0, k * chunk)
                pieces.append((dot_t(qh, kself[back, here]), vself, here, back))
            tip = jnp.where(low, dot_t(qh, kh), -1e30)
            m = jnp.max(tip, axis=1, keepdims=True)
            for sc, _, _, _ in pieces:
                m = jnp.maximum(m, jnp.max(sc, axis=1, keepdims=True))
            w = jnp.exp2((tip - m) * factor)
            l = jnp.sum(w, axis=1, keepdims=True)
            o = dot(w.astype(BF16), vh)
            for sc, ref, cols, part in pieces:
                w = jnp.exp2((sc - m) * factor)
                l = l + jnp.sum(w, axis=1, keepdims=True)
                o = o + dot(w.astype(BF16), ref[part, cols])
            ctx_own[at, here] = (o / l).astype(BF16)
        ctx_swap(k).start()

    loads[1].wait()
    loads[2].wait()
    loads[3].wait()
    prefill(0)

    wait_all(q_copy)
    for g in range(n_req):
        qwide[g * rows : (g + 1) * rows, :] = allq[g].astype(F32)
    begin, size = jnp.int32(0), jnp.int32(0)
    for g in range(n_req):
        begin = begin + jnp.where(g < me, sizes[g], 0)
        size = size + jnp.where(g == me, sizes[g], 0)
    slot = lax.broadcasted_iota(jnp.int32, (GMAX, every), 0)
    rank = lax.broadcasted_iota(jnp.int32, (GMAX, every), 1)
    held = jnp.where((rank == begin + slot) & (slot < size), 1.0, 0.0).astype(BF16)
    named = jnp.where(
        order[...] == lax.broadcasted_iota(jnp.int32, (every, every), 0), 1.0, 0.0
    ).astype(BF16)
    pick = dot_t(held, named).astype(BF16)
    back = dot_t(named, held)
    chosen = dot(pick, qwide[...].astype(BF16)).astype(BF16)
    lane = lax.broadcasted_iota(jnp.int32, (GMAX, 128), 1)
    stat = jnp.zeros((GMAX, 128), F32)
    for h in range(heads):
        here = slice(h * 128, (h + 1) * 128)
        kcol = slice(h * 256, h * 256 + 128)
        vcol = slice(h * 256 + 128, h * 256 + 256)
        sc = dot_t(chosen[:, here], prefix[:, kcol]) * scale
        m = jnp.max(sc, axis=1, keepdims=True)
        w = jnp.exp(sc - m)
        stat = jnp.where(lane == h, m, stat)
        stat = jnp.where(lane == heads + h, jnp.sum(w, axis=1, keepdims=True), stat)
        far[:, here] = dot(w.astype(BF16), prefix[:, vcol])
    far[:, width:] = stat
    spread = jnp.dot(
        back, far[...], preferred_element_type=F32, precision=lax.Precision.HIGHEST
    )
    for g in range(n_req):
        farsend[g] = spread[g * rows : (g + 1) * rows, :]
    start_all(f_copy)
    farrecv[me] = farsend[me]

    for k in range(1, count - 1):
        prefill(k)

    wait_all(f_copy)
    got = farrecv[0]
    for g in range(1, n_req):
        got = got + farrecv[g]
    for h in range(heads):
        here = slice(h * 128, (h + 1) * 128)
        mp, lp = got[:, width + h : width + h + 1], got[:, width + heads + h : width + heads + h + 1]
        ml = near[:, width + h : width + h + 1]
        ll = near[:, width + heads + h : width + heads + h + 1]
        top = jnp.maximum(mp, ml)
        a, b = jnp.exp(mp - top), jnp.exp(ml - top)
        dctx_own[:, here] = ((a * got[:, here] + b * near[:, here]) / (a * lp + b * ll)).astype(BF16)
    dec_swap = swap(dctx_own, dctx_peer, 1)
    dec_swap.start()
    last_swap.wait()
    prefill(count - 1)

    loads[5].wait()
    weight_swap.wait()
    dec_swap.wait()
    dec_out[...] = (
        dot(dctx_own[...], wout_own[...]) + dot(dctx_peer[...], wout_peer[...])
    ).astype(BF16)
    for k in range(count):
        ctx_swap(k).wait()
        at = band(k)
        pre_out[at, :] = (
            dot(ctx_own[at, :], wout_own[...]) + dot(ctx_peer[at, :], wout_peer[...])
        ).astype(BF16)


def places_tables(places):
    lane = jnp.arange(128, dtype=jnp.int32)
    inverse = 10000.0 ** (-((lane & 63).astype(F32) / 64))
    angles = places.astype(F32)[:, None] * inverse[None, :]
    return jnp.cos(angles), jnp.sin(angles) * jnp.where(lane < 64, -1.0, 1.0)[None, :]


def fused(
    n_req, own_dec, own_pre, peer_pre, weight, prefix, pool, flat_out,
    group_sizes, member_order, page_table, cached_len, span_start,
):
    rows, share = own_dec.shape
    block = own_pre.shape[0]
    width = flat_out.shape[0]
    heads = width // 128
    every = n_req * rows
    dcos, dsin = places_tables(prefix.shape[0] + cached_len)
    pcos, psin = places_tables(span_start[0] + jnp.arange(block, dtype=jnp.int32))
    anyw = pl.BlockSpec(memory_space=pl.ANY)
    dma = pltpu.SemaphoreType.DMA
    count = block // CHUNK
    return pl.pallas_call(
        functools.partial(fused_kernel, n_req, heads, 128 ** (-0.5)),
        out_shape=[
            jax.ShapeDtypeStruct((rows, share), BF16),
            jax.ShapeDtypeStruct((block, share), BF16),
        ],
        in_specs=[VM] + [anyw] * 6 + [VM] * 4 + [SM, VM, SM, SM, SM],
        out_specs=[VM, VM],
        scratch_shapes=[
            pltpu.VMEM((rows, share), BF16),
            pltpu.VMEM(weight.shape, BF16),
            pltpu.VMEM((block, share), BF16),
            pltpu.VMEM((block, share), BF16),
            pltpu.VMEM(prefix.shape, BF16),
            pltpu.VMEM(pool.shape, BF16),
            pltpu.VMEM((width, share), BF16),
            pltpu.VMEM((width, share), BF16),
            pltpu.VMEM((block, width), BF16),
            pltpu.VMEM((block, width), BF16),
            pltpu.VMEM((block, width), BF16),
            pltpu.VMEM((block, width), BF16),
            pltpu.VMEM((rows, width), BF16),
            pltpu.VMEM((rows, width), BF16),
            pltpu.VMEM((rows, width), BF16),
            pltpu.VMEM((n_req, rows, width), BF16),
            pltpu.VMEM((every, width), F32),
            pltpu.VMEM((GMAX, width + 128), F32),
            pltpu.VMEM((n_req, rows, width + 128), F32),
            pltpu.VMEM((n_req, rows, width + 128), F32),
            pltpu.VMEM((rows, width + 128), F32),
            dma((6,)),
            dma((n_req,)),
            dma((n_req,)),
            dma((n_req,)),
            dma((n_req,)),
            dma((4 + count,)),
            dma((4 + count,)),
        ],
        compiler_params=pltpu.CompilerParams(
            collective_id=3, has_side_effects=True, vmem_limit_bytes=BIG
        ),
        name="fused",
    )(
        own_dec, own_pre, peer_pre, weight, prefix, pool, flat_out,
        dcos, dsin, pcos, psin, group_sizes, member_order[None, :], page_table.T, cached_len,
        span_start,
    )


def tables(places):
    inverse = 10000.0 ** (-(jnp.arange(64, dtype=F32) / 64))
    angles = places.astype(F32)[:, None] * inverse[None, :]
    c, s = jnp.cos(angles), jnp.sin(angles)
    return jnp.concatenate([c, c], axis=1), jnp.concatenate([-s, s], axis=1)


def local(
    n_req,
    n_tp,
    decode_tokens,
    prefill_tokens,
    qkv_weight,
    out_weight,
    prefix_cache,
    page_pool,
    page_table,
    cached_len,
    group_sizes,
    member_order,
    span_start,
):
    heads = qkv_weight.shape[2]
    width = heads * 128
    features = qkv_weight.shape[0]
    scale = 128 ** (-0.5)
    prefix_len = prefix_cache.shape[1]
    block_rows, share = prefill_tokens.shape
    dec_count = decode_tokens.shape[0]
    me = lax.axis_index("req")
    side = lax.axis_index("tp")
    swap = [(0, 1), (1, 0)]
    joined = n_tp == 2 and block_rows % CHUNK == 0 and block_rows > CHUNK
    if joined:
        head = prefill_tokens[: block_rows - CHUNK]
        head = lax.ppermute(head, "tp", swap)
        offs = [side * share, (1 - side) * share]
    elif n_tp == 2:
        dec_parts = [decode_tokens, lax.ppermute(decode_tokens, "tp", swap)]
        pre_parts = [prefill_tokens, lax.ppermute(prefill_tokens, "tp", swap)]
        offs = [side * share, (1 - side) * share]
    else:
        dec_parts = [lax.all_gather(decode_tokens, "tp", axis=1, tiled=True)]
        pre_parts = [lax.all_gather(prefill_tokens, "tp", axis=1, tiled=True)]
        offs = [jnp.int32(0)]
    n = len(offs)
    slots = page_pool.shape[0] * page_pool.shape[1]
    weight, prefix, pool = prep(
        [
            qkv_weight.reshape(-1, 128),
            prefix_cache.reshape(-1, 128),
            page_pool.reshape(-1, 128),
        ],
        [3 * heads, 2 * heads, 2 * heads],
        features,
    ) if features == prefix_len == slots else (
        prep([qkv_weight.reshape(-1, 128)], [3 * heads], features)
        + prep([prefix_cache.reshape(-1, 128)], [2 * heads], prefix_len)
        + prep([page_pool.reshape(-1, 128)], [2 * heads], slots)
    )
    if joined:
        dec_out, pre_out = fused(
            n_req, decode_tokens, prefill_tokens, head, weight, prefix, pool,
            out_weight.reshape(width, out_weight.shape[2]),
            group_sizes, member_order, page_table, cached_len, span_start,
        )
        return (dec_out, pre_out)
    begin = jnp.cumsum(group_sizes) - group_sizes
    slot_at = jnp.arange(GMAX, dtype=jnp.int32)[None, :]
    padded = jnp.concatenate([member_order, jnp.zeros((GMAX,), jnp.int32)])
    owners = jnp.where(
        slot_at < group_sizes[:, None], padded[begin[:, None] + slot_at], -1
    )
    members = lax.dynamic_slice_in_dim(owners, me, 1, axis=0).reshape(GMAX, 1)
    dcos, dsin = tables(prefix_len + cached_len)
    pcos, psin = tables(span_start[0] + jnp.arange(block_rows, dtype=jnp.int32))
    off_arr = jnp.stack(offs).astype(jnp.int32)
    row = jax.ShapeDtypeStruct((dec_count, width), BF16)
    dq, dk, dv = pl.pallas_call(
        functools.partial(dec_qkv_kernel, n, heads),
        out_shape=[row, row, row],
        in_specs=[SM] + [VM] * (n + 3),
        out_specs=[VM] * 3,
        compiler_params=pltpu.CompilerParams(vmem_limit_bytes=BIG),
        name="dec_qkv",
    )(off_arr, *dec_parts, weight, dcos, dsin)
    allq = gather_all(dq, "req", n_req, 1).reshape(n_req * dec_count, width)
    far, near = pl.pallas_call(
        functools.partial(dec_attn_kernel, heads, scale),
        out_shape=[
            jax.ShapeDtypeStruct((GMAX, width + 128), F32),
            jax.ShapeDtypeStruct((dec_count, width + 128), F32),
        ],
        in_specs=[VM] * 9,
        out_specs=[VM] * 2,
        compiler_params=pltpu.CompilerParams(vmem_limit_bytes=BIG),
        name="dec_attn",
    )(allq, members, prefix, dq, dk, dv, pool, page_table, cached_len[:, None])
    got = gather_all(far, "req", n_req, 2).reshape(n_req * GMAX, width + 128)
    dec_ctx = pl.pallas_call(
        functools.partial(merge_kernel, heads),
        out_shape=row,
        in_specs=[SM] + [VM] * 3,
        out_specs=VM,
        compiler_params=pltpu.CompilerParams(vmem_limit_bytes=BIG),
        name="merge",
    )((me * dec_count)[None].astype(jnp.int32), got, owners.reshape(1, -1), near)
    flat_out = out_weight.reshape(width, out_weight.shape[2])
    if n_tp == 2:
        theirs = lax.dynamic_slice_in_dim(flat_out, (1 - side) * share, share, axis=1)
        theirs, pre_parts[1] = lax.optimization_barrier((theirs, pre_parts[1]))
        peer_w = lax.ppermute(theirs, "tp", swap)
        own_w = lax.dynamic_slice_in_dim(flat_out, side * share, share, axis=1)
    chunk = min(128, block_rows)
    scal = jnp.concatenate([off_arr, span_start]).astype(jnp.int32)
    whole = lambda a: pl.BlockSpec(a.shape, lambda i: (0, 0), pipeline_mode=pl.Buffered(1))
    band = lambda w: pl.BlockSpec((chunk, w), lambda i: (i, 0))
    pre_ctx = pl.pallas_call(
        functools.partial(prefill_kernel, n, heads, chunk, scale),
        grid=(block_rows // chunk,),
        out_shape=jax.ShapeDtypeStruct((block_rows, width), BF16),
        in_specs=[SM]
        + [band(p.shape[1]) for p in pre_parts]
        + [whole(weight), band(128), band(128), whole(prefix)],
        out_specs=band(width),
        scratch_shapes=[pltpu.VMEM((block_rows, width), BF16)] * 2,
        compiler_params=pltpu.CompilerParams(vmem_limit_bytes=BIG),
        cost_estimate=pl.CostEstimate(
            flops=int(8e9), bytes_accessed=int(13e6), transcendentals=int(5e6)
        ),
        name="prefill",
    )(scal, *pre_parts, weight, pcos, psin, prefix)
    if n_tp == 2:
        pre_ctxs = [pre_ctx, lax.ppermute(pre_ctx, "tp", swap)]
        dec_ctxs = [dec_ctx, lax.ppermute(dec_ctx, "tp", swap)]
        outs_w, kind = [own_w, peer_w], BF16
    else:
        pre_ctxs, dec_ctxs, outs_w, kind = [pre_ctx], [dec_ctx], [flat_out], F32
    m = len(outs_w)
    span = outs_w[0].shape[1]
    pre_out, dec_out = pl.pallas_call(
        functools.partial(out_kernel, m),
        grid=(block_rows // chunk,),
        out_shape=[
            jax.ShapeDtypeStruct((block_rows, span), kind),
            jax.ShapeDtypeStruct((dec_count, span), kind),
        ],
        in_specs=[band(width)] * m + [whole(d) for d in dec_ctxs] + [whole(w) for w in outs_w],
        out_specs=[band(span), pl.BlockSpec((dec_count, span), lambda i: (0, 0))],
        compiler_params=pltpu.CompilerParams(vmem_limit_bytes=BIG),
        name="out_proj",
    )(*pre_ctxs, *dec_ctxs, *outs_w)
    if n_tp != 2:
        dec_out = lax.psum_scatter(dec_out, "tp", scatter_dimension=1, tiled=True).astype(BF16)
        pre_out = lax.psum_scatter(pre_out, "tp", scatter_dimension=1, tiled=True).astype(BF16)
    return (dec_out, pre_out)


def solution(mesh):
    placed = (
        P("req", "tp"),
        P("req", "tp"),
        P(None, None, "tp", None),
        P("tp", None, None),
        P("req", None, "tp", None, None),
        P("req", None, "tp", None, None),
        P("req", None),
        P("req"),
        P(),
        P(),
        P("req"),
    )
    return jax.shard_map(
        functools.partial(local, mesh.shape["req"], mesh.shape["tp"]),
        mesh=mesh,
        in_specs=placed,
        out_specs=(P("req", "tp"), P("req", "tp")),
        check_vma=False,
    )
```
